32 devices in a mesh: groups: 2 (over y), seq: 8 (over z, x), head: 2 (over core).
Axes of the slice: x: 2, y: 2, z: 4, core: 2. Of those that a mesh axis runs over, the one named last changes fastest.
Arguments:
- queries: bfloat16 [4096, 4096], P(('groups', 'seq'), 'head'), parts along dimension 0, may hold values from -40 to 40
- key_vectors: bfloat16 [4096, 4096], P(('groups', 'seq'), 'head'), parts along dimension 0, may hold values from -6 to 6
- value_vectors: bfloat16 [4096, 4096], P(('groups', 'seq'), 'head'), parts along dimension 0, may hold values from -40 to 40
- output_grad: bfloat16 [4096, 4096], P(('groups', 'seq'), 'head'), parts along dimension 0, may hold values from -6 to 6
- norm_gain: float32 [4096], P('head'), may hold values from 0.5 to 2
- block_docs: int32 [16], P(('groups', 'seq')), parts along dimension 0, may hold values from 0 to 3, never falling along the last dimension, each value on 1 to 4 neighbouring positions
Outputs:
- normed: bfloat16 [4096, 4096], P(('groups', 'seq'), 'head'), parts along dimension 0
- query_grad: bfloat16 [4096, 4096], P(('groups', 'seq'), 'head'), parts along dimension 0
- key_grad: bfloat16 [4096, 4096], P(('groups', 'seq'), 'head'), parts along dimension 0
- value_grad: bfloat16 [4096, 4096], P(('groups', 'seq'), 'head'), parts along dimension 0
The draws below stay inside these ranges and needn't reach their ends.
There are 2 independent parts, one for each index of `groups`. The reference program is written for one: setup_inputs(seed, part) draws one part's arguments, and reference() takes and returns one part's arrays. A program takes and returns all parts, laid end to end along the dimension named above; an argument that names none is the same for every part. Nothing has to cross between parts.
Inputs may be any that keep to these rules, and one draw needn't show every extreme that they name: `block_docs`: block document ids never fall along the sequence; every one of the 4 documents covers 1 to 4 blocks, and one covers exactly 4.
All inputs are finite; a program needn't handle non-finite values.
Results may differ from the reference program's by a relative error of at most 0.0058.
Values sent between devices are 32-bit elements; how exact they have to be, the bound alone decides.
No kernel may reach another device: no remote copies, remote signals or barrier semaphores. Data moves between devices by JAX's collectives and lax.ppermute only.
A program may use at most 64 MiB of HBM per device.

```python
import math
import jax
import jax.numpy as jnp
import numpy as np
from jax import lax

HEADS = 32
HEAD_DIM = 128
BLOCK = 256
DOCS = 4
WIDTH = 4096
LENGTH = 2048
NBLK = 8


def draw_queries(key, part):
    base_key = jax.random.fold_in(key, 11)
    scale_key = jax.random.fold_in(key, 12)
    row_scale = jnp.exp(jax.random.uniform(scale_key, (LENGTH, 1), jnp.float32, 0.0, math.log(10.0)))
    base = jnp.clip(jax.random.normal(base_key, (LENGTH, WIDTH), jnp.float32), -4.0, 4.0)
    return (base * row_scale).astype(jnp.bfloat16)


def draw_value_vectors(key, part):
    base_key = jax.random.fold_in(key, 21)
    scale_key = jax.random.fold_in(key, 22)
    head_scale = jnp.exp(jax.random.uniform(scale_key, (HEADS,), jnp.float32, 0.0, math.log(10.0)))
    column_scale = jnp.repeat(head_scale, HEAD_DIM)[None, :]
    base = jnp.clip(jax.random.normal(base_key, (LENGTH, WIDTH), jnp.float32), -4.0, 4.0)
    return (base * column_scale).astype(jnp.bfloat16)


def level_of(key, dims, cuts, least, high):
    def one(axis_at, parts):
        heights = jax.random.uniform(jax.random.fold_in(jax.random.fold_in(key, 6), axis_at), (parts,), jnp.float32, least / len(cuts), high / len(cuts))
        return jnp.repeat(jnp.exp(heights), dims[axis_at] // parts).reshape((-1,) + (1,) * (len(dims) - axis_at - 1))

    gain = one(*cuts[0])
    for cut in cuts[1:]:
        gain = gain * one(*cut)
    return gain


def profile(number_of, total, limit, lean):
    weights = [(1 << 20) // math.isqrt(rank ** lean) + 1 for rank in range(2, number_of + 1)]
    spare, holding = total - limit - (number_of - 1), [1] * (number_of - 1)
    while spare > 0:
        candidates = [i for i in range(number_of - 1) if holding[i] < limit]
        whole, remaining = sum([weights[i] for i in candidates]), spare
        for i in candidates:
            addition = min(limit - holding[i], max(1, remaining * weights[i] // whole), spare)
            holding[i] = holding[i] + addition
            spare = spare - addition
    return np.array([limit] + holding)


def uneven_parts(rng, amount, total, bound, slope):
    if amount == 2:
        one = jax.random.randint(rng, (), max(1, total - bound), min(bound, total - 1) + 1)
        return jnp.stack([one, total - one])
    tallies = jnp.asarray(profile(amount, total, bound, slope), jnp.int32)
    couples = (amount - 1) // 2
    giver, taker = tallies[1:1 + 2 * couples:2], tallies[2:2 + 2 * couples:2]
    room = jnp.minimum(giver - 1, bound - taker)
    passed = jax.random.randint(jax.random.fold_in(rng, 1), (couples,), 0, 1 << 20) % (room + 1)
    tallies = tallies.at[1:1 + 2 * couples:2].set(giver - passed).at[2:2 + 2 * couples:2].set(taker + passed)
    return tallies[jax.random.permutation(jax.random.fold_in(rng, 2), amount)]


def centred(key, extent, deviation, most, cuts=(), held_as=jnp.bfloat16):
    drawn = deviation * jax.random.normal(key, extent, jnp.float32)
    if cuts:
        drawn = drawn * level_of(key, extent, cuts, -0.22, 0.18)
    return jnp.clip(drawn, -most, most).astype(held_as)


def setup_inputs(seed: int = 0, part: int = 0) -> dict:
    key_list = jax.random.split(jax.random.key(seed), 7)
    own_keys = jax.random.split(jax.random.fold_in(key_list[6], part), 7)
    return {
        "queries": draw_queries(jax.random.fold_in(jax.random.fold_in(key_list[6], part), 71), part),
        "key_vectors": centred(own_keys[1], (LENGTH, WIDTH), 1.0, 6.0, ((0, 8), (1, 2))),
        "value_vectors": draw_value_vectors(jax.random.fold_in(jax.random.fold_in(key_list[6], part), 71), part),
        "output_grad": centred(own_keys[3], (LENGTH, WIDTH), 1.0, 6.0, ((0, 8), (1, 2))),
        "norm_gain": jnp.clip(jnp.exp(math.log(2.0) - 1.3862944 * jax.random.uniform(key_list[4], (WIDTH,), jnp.float32) ** level_of(key_list[4], (WIDTH,), ((0, 2),), -0.2, 0.2)), 0.5, 2.0),
        "block_docs": jnp.searchsorted(jnp.cumsum(uneven_parts(own_keys[5], DOCS, NBLK, NBLK // 2, 0)), jnp.arange(NBLK), side="right").astype(jnp.int32),
    }


norm_eps = 1e-06

def rounded(array):
    return lax.optimization_barrier(array.astype(jnp.bfloat16)).astype(jnp.float32)

def reference(queries, key_vectors, value_vectors, output_grad, norm_gain, block_docs):
    nblocks = block_docs.shape[0]
    shape_four = (nblocks, BLOCK, HEADS, HEAD_DIM)
    query_blk = queries.astype(jnp.float32).reshape(shape_four)
    key_blk = key_vectors.astype(jnp.float32).reshape(shape_four)
    value_blk = value_vectors.astype(jnp.float32).reshape(shape_four)
    block_kv = jnp.einsum('bshd,bshe->bhde', key_blk, value_blk)
    position = lax.iota(jnp.int32, nblocks)
    same_doc = block_docs[:, None] == block_docs[None, :]
    earlier = (same_doc & (position[None, :] < position[:, None])).astype(jnp.float32)
    later = (same_doc & (position[None, :] > position[:, None])).astype(jnp.float32)
    states_in = rounded(jnp.einsum('bc,chde->bhde', earlier, block_kv, precision=lax.Precision.HIGHEST))
    tok_pos = lax.iota(jnp.int32, BLOCK)
    causal = (tok_pos[:, None] >= tok_pos[None, :]).astype(jnp.float32)

    def forward_block(pieces):
        query_one, key_one, value_one, state_one = pieces
        scores = jnp.einsum('thd,shd->hts', query_one, key_one) * causal[None]
        att_weights = rounded(scores)
        attended = jnp.einsum('hts,she->the', att_weights, value_one) + jnp.einsum('thd,hde->the', query_one, state_one)
        return attended.reshape(BLOCK, HEADS * HEAD_DIM)
    attended = lax.map(forward_block, (query_blk, key_blk, value_blk, states_in)).reshape(-1, HEADS * HEAD_DIM)
    full_width = HEADS * HEAD_DIM
    scaled_grad = norm_gain[None, :] * output_grad.astype(jnp.float32)
    inverse_rms = lax.rsqrt(lax.optimization_barrier(jnp.sum(attended * attended, axis=1)) / full_width + norm_eps)
    cross_sum = lax.optimization_barrier(jnp.sum(attended * scaled_grad, axis=1))
    normed = (attended * inverse_rms[:, None] * norm_gain[None, :]).astype(jnp.bfloat16)
    attended_grad = inverse_rms[:, None] * scaled_grad - attended * (inverse_rms ** 3 * cross_sum / full_width)[:, None]
    grad_blk = rounded(attended_grad).reshape(shape_four)
    block_grad = jnp.einsum('bthd,bthe->bhde', query_blk, grad_blk)
    grads_in = rounded(jnp.einsum('bc,chde->bhde', later, block_grad, precision=lax.Precision.HIGHEST))

    def backward_block(pieces):
        query_one, key_one, value_one, grad_one, state_one, incoming = pieces
        att_weights = rounded(jnp.einsum('thd,shd->hts', query_one, key_one) * causal[None])
        grad_weights = rounded(jnp.einsum('the,she->hts', grad_one, value_one) * causal[None])
        query_part = jnp.einsum('hts,shd->thd', grad_weights, key_one) + jnp.einsum('the,hde->thd', grad_one, state_one)
        key_part = jnp.einsum('hts,thd->shd', grad_weights, query_one) + jnp.einsum('she,hde->shd', value_one, incoming)
        value_part = jnp.einsum('hts,the->she', att_weights, grad_one) + jnp.einsum('shd,hde->she', key_one, incoming)
        return (query_part.astype(jnp.bfloat16), key_part.astype(jnp.bfloat16), value_part.astype(jnp.bfloat16))
    query_grad, key_grad, value_grad = lax.map(backward_block, (query_blk, key_blk, value_blk, grad_blk, states_in, grads_in))
    flat_shape = (nblocks * BLOCK, HEADS * HEAD_DIM)
    return (normed, query_grad.reshape(flat_shape), key_grad.reshape(flat_shape), value_grad.reshape(flat_shape))
```

```python
import functools

import jax
import jax.numpy as jnp
from jax import lax
from jax.experimental import pallas as pl
from jax.experimental.pallas import tpu as pltpu
from jax.sharding import PartitionSpec as P

HEAD_DIM = 128
norm_eps = 1e-06
BF = jnp.bfloat16
F32 = jnp.float32


def spread_prefix(element, weights):
    seq_count = lax.axis_size("seq")
    flat_state = element.reshape(seq_count, -1, element.shape[-1])
    mixed = jnp.einsum(
        "ds,skc->dkc",
        weights,
        lax.all_to_all(flat_state, "seq", split_axis=0, concat_axis=0, tiled=True),
        precision=lax.Precision.HIGHEST,
    )
    returned = lax.all_to_all(mixed, "seq", split_axis=0, concat_axis=0, tiled=True)
    return returned.reshape(element.shape)


def general_body(queries, key_vectors, value_vectors, output_grad, norm_gain, block_docs):
    tokens, local_width = queries.shape
    heads_here = local_width // HEAD_DIM
    nblocks = block_docs.shape[0]
    block_len = tokens // nblocks
    shape_four = (nblocks, block_len, heads_here, HEAD_DIM)
    query_blk = queries.reshape(shape_four)
    key_blk = key_vectors.reshape(shape_four)
    value_blk = value_vectors.reshape(shape_four)
    tok_pos = lax.iota(jnp.int32, block_len)
    causal = (tok_pos[:, None] >= tok_pos[None, :])[None, None]
    scores = jnp.einsum("bthd,bshd->bhts", query_blk, key_blk, preferred_element_type=F32)
    att_weights = jnp.where(causal, scores, 0.0).astype(BF)
    intra_out = jnp.einsum("bhts,bshe->bthe", att_weights, value_blk, preferred_element_type=F32)
    block_kv = jnp.einsum("bshd,bshe->bhde", key_blk, value_blk, preferred_element_type=F32)
    position = lax.iota(jnp.int32, nblocks)
    same_doc = block_docs[:, None] == block_docs[None, :]
    earlier_mask = (same_doc & (position[None, :] < position[:, None])).astype(F32)
    later_mask = (same_doc & (position[None, :] > position[:, None])).astype(F32)
    local_in = jnp.einsum("kj,jhde->khde", earlier_mask, block_kv, precision=lax.Precision.HIGHEST)
    tail_weight = (block_docs == block_docs[-1]).astype(F32)
    tail_state = jnp.einsum("j,jhde->hde", tail_weight, block_kv, precision=lax.Precision.HIGHEST)
    seq_count = lax.axis_size("seq")
    all_docs = lax.all_gather(block_docs, "seq", axis=0, tiled=True).reshape(seq_count, nblocks)
    first_all = all_docs[:, 0]
    last_all = all_docs[:, -1]
    source_pos = lax.iota(jnp.int32, seq_count)
    forward_weights = (
        (source_pos[None, :] < source_pos[:, None]) & (last_all[None, :] == first_all[:, None])
    ).astype(F32)
    backward_weights = (
        (source_pos[None, :] > source_pos[:, None]) & (first_all[None, :] == last_all[:, None])
    ).astype(F32)
    carry_state = spread_prefix(tail_state, forward_weights)
    carry_use = block_docs == block_docs[0]
    states_in = (
        local_in + jnp.where(carry_use[:, None, None, None], carry_state[None], 0.0)
    ).astype(BF)
    inter_out = jnp.einsum("bthd,bhde->bthe", query_blk, states_in, preferred_element_type=F32)
    attended = (intra_out + inter_out).reshape(tokens, local_width)
    scaled_grad = norm_gain[None, :] * output_grad.astype(F32)
    square_sum, cross_sum = lax.psum(
        (jnp.sum(attended * attended, axis=1), jnp.sum(attended * scaled_grad, axis=1)), "head"
    )
    full_width = local_width * lax.axis_size("head")
    inverse_rms = lax.rsqrt(square_sum / full_width + norm_eps)
    normed = (attended * inverse_rms[:, None] * norm_gain[None, :]).astype(BF)
    attended_grad = (
        inverse_rms[:, None] * scaled_grad
        - attended * (inverse_rms**3 * cross_sum / full_width)[:, None]
    )
    grad_blk = attended_grad.astype(BF).reshape(shape_four)
    score_grad = jnp.einsum("bthe,bshe->bhts", grad_blk, value_blk, preferred_element_type=F32)
    grad_weights = jnp.where(causal, score_grad, 0.0).astype(BF)
    query_part = jnp.einsum("bhts,bshd->bthd", grad_weights, key_blk, preferred_element_type=F32)
    query_part = query_part + jnp.einsum(
        "bthe,bhde->bthd", grad_blk, states_in, preferred_element_type=F32
    )
    key_intra = jnp.einsum("bhts,bthd->bshd", grad_weights, query_blk, preferred_element_type=F32)
    value_intra = jnp.einsum("bhts,bthe->bshe", att_weights, grad_blk, preferred_element_type=F32)
    block_grad = jnp.einsum("bthd,bthe->bhde", query_blk, grad_blk, preferred_element_type=F32)
    grad_local = jnp.einsum(
        "kj,jhde->khde", later_mask, block_grad, precision=lax.Precision.HIGHEST
    )
    head_weight = (block_docs == block_docs[0]).astype(F32)
    head_state = jnp.einsum("j,jhde->hde", head_weight, block_grad, precision=lax.Precision.HIGHEST)
    grad_state = spread_prefix(head_state, backward_weights)
    grad_use = block_docs == block_docs[-1]
    grads_in = (
        grad_local + jnp.where(grad_use[:, None, None, None], grad_state[None], 0.0)
    ).astype(BF)
    key_part = key_intra + jnp.einsum(
        "bshe,bhde->bshd", value_blk, grads_in, preferred_element_type=F32
    )
    value_part = value_intra + jnp.einsum(
        "bshd,bhde->bshe", key_blk, grads_in, preferred_element_type=F32
    )
    flat_shape = (tokens, local_width)
    return (
        normed,
        query_part.reshape(flat_shape).astype(BF),
        key_part.reshape(flat_shape).astype(BF),
        value_part.reshape(flat_shape).astype(BF),
    )


HALVES = 2
STEPS = 4
VMEM_LIMIT = 48 * 1024 * 1024


def nn(a, b):
    return lax.dot_general(a, b, (((1,), (0,)), ((), ())), preferred_element_type=F32)


def nt(a, b):
    return lax.dot_general(a, b, (((1,), (1,)), ((), ())), preferred_element_type=F32)


def tn(a, b):
    return lax.dot_general(a, b, (((0,), (0,)), ((), ())), preferred_element_type=F32)


def cols(j):
    return slice(j * HEAD_DIM, (j + 1) * HEAD_DIM)


def own_tag(doc_ref):
    return (doc_ref[0] + 1).astype(F32)


def message_slabs(heads):
    return heads * HEAD_DIM // 8 + 1


def put_head(out_ref, head, value):
    out_ref[pl.ds(head * 16, 16)] = value.reshape(16, 8, HEAD_DIM)


def put_tag(out_ref, doc_ref):
    out_ref[out_ref.shape[0] - 1] = jnp.full((8, HEAD_DIM), own_tag(doc_ref), F32)


def kv_kernel(per, doc_ref, k_ref, v_ref, out_ref):
    i = pl.program_id(0)
    for j in range(per):
        put_head(out_ref, i * per + j, tn(k_ref[:, cols(j)], v_ref[:, cols(j)]))

    @pl.when(i == 0)
    def _():
        put_tag(out_ref, doc_ref)


def lower(n):
    return lax.broadcasted_iota(jnp.int32, (n, n), 0) >= lax.broadcasted_iota(jnp.int32, (n, n), 1)


def intra_kernel(per, q_ref, k_ref, v_ref, att_ref, out_ref):
    mask = lower(q_ref.shape[0])
    for j in range(per):
        scores = nt(q_ref[:, cols(j)], k_ref[:, cols(j)])
        att = jnp.where(mask, scores, 0.0).astype(BF)
        att_ref[j] = att
        out_ref[:, cols(j)] = nn(att, v_ref[:, cols(j)])


def gathered(head, doc_ref, flag_ref, r1_ref, r2_ref, r3_ref):
    own = own_tag(doc_ref)
    last = r1_ref.shape[0] - 1
    use3 = flag_ref[0]
    m1 = ((r1_ref[last] == own) & (use3 == 0)).astype(F32)
    m2 = (r2_ref[last] == own).astype(F32)
    m3 = ((r3_ref[last] == own) & (use3 == 1)).astype(F32)
    at = pl.ds(head * 16, 16)
    total = r2_ref[at] * m2 + r1_ref[at] * m1 + r3_ref[at] * m3
    return total.reshape(HEAD_DIM, HEAD_DIM).astype(BF)


def attend_kernel(per, last_half, doc_ref, flag_ref, q_ref, intra_ref, do_ref, gain_ref, r1_ref, r2_ref, r3_ref, *rest):
    if last_half:
        sum_in_ref, att_ref, state_ref, sum_ref, acc_ref = rest
    else:
        att_ref, state_ref, sum_ref, acc_ref = rest
    i = pl.program_id(0)

    @pl.when(i == 0)
    def _():
        if last_half:
            acc_ref[...] = sum_in_ref[...]
        else:
            acc_ref[...] = jnp.zeros_like(acc_ref)

    square = acc_ref[0]
    cross = acc_ref[1]
    for j in range(per):
        state = gathered(i * per + j, doc_ref, flag_ref, r1_ref, r2_ref, r3_ref)
        state_ref[j] = state
        att = intra_ref[:, cols(j)] + nn(q_ref[:, cols(j)], state)
        att_ref[:, cols(j)] = att
        square = square + att * att
        cross = cross + att * (gain_ref[:, cols(j)] * do_ref[:, cols(j)].astype(F32))
    acc_ref[0] = square
    acc_ref[1] = cross

    @pl.when(i == pl.num_programs(0) - 1)
    def _():
        if last_half:
            lane = lax.broadcasted_iota(jnp.int32, square.shape, 1)
            sq = jnp.sum(square, axis=1, keepdims=True)
            cr = jnp.sum(cross, axis=1, keepdims=True)
            sum_ref[...] = jnp.where(lane == 0, sq, jnp.where(lane == 1, cr, 0.0))
        else:
            sum_ref[0] = square
            sum_ref[1] = cross


def scales(mine_ref, other_ref, width):
    total = mine_ref[...] + other_ref[...]
    inverse = lax.rsqrt(total[:, 0:1] / width + norm_eps)
    coef = inverse * inverse * inverse * total[:, 1:2] / width
    return inverse, coef


def grad_kernel(per, width, doc_ref, q_ref, att_ref, do_ref, gain_ref, mine_ref, other_ref, ag_ref, out_ref):
    i = pl.program_id(0)
    inverse, coef = scales(mine_ref, other_ref, width)
    for j in range(per):
        scaled = gain_ref[:, cols(j)] * do_ref[:, cols(j)].astype(F32)
        ag = (inverse * scaled - att_ref[:, cols(j)] * coef).astype(BF)
        ag_ref[:, cols(j)] = ag
        put_head(out_ref, i * per + j, tn(q_ref[:, cols(j)], ag))

    @pl.when(i == 0)
    def _():
        put_tag(out_ref, doc_ref)


def back_kernel(per, width, q_ref, k_ref, v_ref, ag_ref, atw_ref, state_ref, att_ref, gain_ref, mine_ref, other_ref, *rest):
    normed_ref, qg_ref, kin_ref, vin_ref = rest[-4:]
    inverse, _ = scales(mine_ref, other_ref, width)
    mask = lower(q_ref.shape[0])
    for j in range(per):
        q = q_ref[:, cols(j)]
        ag = ag_ref[:, cols(j)]
        normed_ref[:, cols(j)] = (att_ref[:, cols(j)] * inverse * gain_ref[:, cols(j)]).astype(BF)
        gw = jnp.where(mask, nt(ag, v_ref[:, cols(j)]), 0.0).astype(BF)
        qg_ref[:, cols(j)] = (nn(gw, k_ref[:, cols(j)]) + nt(ag, state_ref[j])).astype(BF)
        kin_ref[:, cols(j)] = tn(gw, q)
        vin_ref[:, cols(j)] = tn(atw_ref[j], ag)


def final_kernel(per, doc_ref, flag_ref, k_ref, v_ref, kin_ref, vin_ref, r1_ref, r2_ref, r3_ref, *rest):
    kg_ref, vg_ref = rest[-2:]
    i = pl.program_id(0)
    for j in range(per):
        grads = gathered(i * per + j, doc_ref, flag_ref, r1_ref, r2_ref, r3_ref)
        kg_ref[:, cols(j)] = (kin_ref[:, cols(j)] + nt(v_ref[:, cols(j)], grads)).astype(BF)
        vg_ref[:, cols(j)] = (vin_ref[:, cols(j)] + nn(k_ref[:, cols(j)], grads)).astype(BF)


def call(kernel, name, in_specs, out_specs, out_shape, scratch=(), aliases=None, flops=0, steps=STEPS):
    return pl.pallas_call(
        kernel,
        grid=(steps,),
        in_specs=in_specs,
        out_specs=out_specs,
        out_shape=out_shape,
        scratch_shapes=list(scratch),
        input_output_aliases=aliases or {},
        name=name,
        cost_estimate=pl.CostEstimate(flops=flops, transcendentals=0, bytes_accessed=4 << 20),
        compiler_params=pltpu.CompilerParams(
            dimension_semantics=("arbitrary",), vmem_limit_bytes=VMEM_LIMIT
        ),
    )


def pairs_of(seq, head, rule):
    out = []
    for s in range(seq):
        for h in range(head):
            to = rule(s, h)
            if to is not None and 0 <= to < seq:
                out.append((s * head + h, to * head + h))
    return out


def routes(seq, head, sign):
    first = pairs_of(seq, head, lambda s, h: s ^ 1 if h % 2 == 0 else s + 2 * sign)
    second = pairs_of(seq, head, lambda s, h: s + 2 * sign if h % 2 == 0 else s + sign)
    parity = 0 if sign > 0 else 1
    third = pairs_of(
        seq, head, lambda s, h: s + 2 * sign if h % 2 == 0 and s % 2 == parity else None
    )
    return first, second, third


def send(x, pairs):
    return lax.ppermute(x, ("seq", "head"), pairs)


def join_kernel(role_ref, own_ref, got_ref, out_ref):
    last = own_ref.shape[0] - 1
    same = (own_ref[last] == got_ref[last]).astype(F32)

    @pl.when(role_ref[0] == 1)
    def _():
        out_ref[...] = got_ref[...] + own_ref[...] * same[None]
        out_ref[last] = got_ref[last]

    @pl.when(role_ref[0] == 0)
    def _():
        out_ref[...] = own_ref[...] + got_ref[...] * same[None]
        out_ref[last] = own_ref[last]


def block_body(queries, key_vectors, value_vectors, output_grad, norm_gain, block_docs):
    tokens, width = queries.shape
    heads = width // HEAD_DIM
    seq = lax.axis_size("seq")
    head = lax.axis_size("head")
    full = width * head
    hh = heads // HALVES
    steps = STEPS
    per = hh // steps
    pw = per * HEAD_DIM
    hw = hh * HEAD_DIM
    gain = norm_gain.reshape(1, width)
    seq_at = lax.axis_index("seq")
    core_at = lax.axis_index("head")
    even_core = core_at % 2 == 0
    odd_block = seq_at % 2 == 1
    smem = pl.BlockSpec(memory_space=pltpu.SMEM)
    slabs = message_slabs(hh)
    message = jax.ShapeDtypeStruct((slabs, 8, HEAD_DIM), F32)
    whole = pl.BlockSpec((slabs, 8, HEAD_DIM), lambda i: (0, 0, 0))
    sums_spec = pl.BlockSpec((tokens, HEAD_DIM), lambda i: (0, 0))
    local = pl.BlockSpec((tokens, pw), lambda i: (0, i))
    square = pl.BlockSpec((per, tokens, tokens), lambda i: (i, 0, 0))
    states = pl.BlockSpec((per, HEAD_DIM, HEAD_DIM), lambda i: (i, 0, 0))
    acc_shape = jax.ShapeDtypeStruct((2, tokens, HEAD_DIM), F32)
    acc_spec = pl.BlockSpec((2, tokens, HEAD_DIM), lambda i: (0, 0, 0))
    untouched = pl.BlockSpec(memory_space=pl.ANY)
    wide = jax.ShapeDtypeStruct((tokens, width), BF)
    half32 = jax.ShapeDtypeStruct((tokens, hw), F32)

    def part(n):
        return pl.BlockSpec((tokens, pw), lambda i: (0, i + n * steps))

    def gain_part(n):
        return pl.BlockSpec((1, pw), lambda i: (0, i + n * steps))

    mm = 2 * tokens * HEAD_DIM * HEAD_DIM * hh

    def exchange(messages, sign):
        first, second, third = routes(seq, head, sign)
        low_block = odd_block if sign < 0 else ~odd_block
        got1 = [send(m, first) for m in messages]
        use3 = (even_core & low_block).astype(jnp.int32).reshape(1)
        on = [
            call(join_kernel, f"join{n}", [smem, whole, whole], whole, message, steps=1)(use3, m, g)
            for n, (m, g) in enumerate(zip(messages, got1))
        ]
        got2 = [send(m, second) for m in on]
        got3 = [send(g, third) for g in got2]
        return use3, list(zip(got1, got2, got3))

    kv = [
        call(functools.partial(kv_kernel, per), f"kv{n}", [smem, part(n), part(n)], whole, message, flops=mm)(
            block_docs, key_vectors, value_vectors
        )
        for n in range(HALVES)
    ]
    use3, got = exchange(kv, 1)
    intra = [
        call(
            functools.partial(intra_kernel, per), f"intra{n}",
            [part(n)] * 3, [square, local],
            [jax.ShapeDtypeStruct((hh, tokens, tokens), BF), half32], flops=4 * mm,
        )(queries, key_vectors, value_vectors)
        for n in range(HALVES)
    ]
    attended, state, sums = [], [], None
    for n in range(HALVES):
        last = n == HALVES - 1
        extra = [acc_spec] if n else []
        att, st, sums = call(
            functools.partial(attend_kernel, per, last), f"attend{n}",
            [smem, smem, part(n), local, part(n), gain_part(n), whole, whole, whole] + extra,
            [local, states, sums_spec if last else acc_spec],
            [
                half32,
                jax.ShapeDtypeStruct((hh, HEAD_DIM, HEAD_DIM), BF),
                jax.ShapeDtypeStruct((tokens, HEAD_DIM), F32) if last else acc_shape,
            ],
            scratch=[pltpu.VMEM((2, tokens, HEAD_DIM), F32)], flops=mm,
        )(block_docs, use3, queries, intra[n][1], output_grad, gain, *got[n], *([sums] if n else []))
        attended.append(att)
        state.append(st)
    other = lax.ppermute(sums, "head", [(c, c ^ 1) for c in range(head)])
    ag, bg = [], []
    for n in range(HALVES):
        a, b = call(
            functools.partial(grad_kernel, per, full), f"grad{n}",
            [smem, part(n), local, part(n), gain_part(n), sums_spec, sums_spec],
            [local, whole], [jax.ShapeDtypeStruct((tokens, hw), BF), message], flops=mm,
        )(block_docs, queries, attended[n], output_grad, gain, sums, other)
        ag.append(a)
        bg.append(b)
    use3b, gotb = exchange(bg, -1)
    kin, vin, normed, query_grad = [], [], None, None
    for n in range(HALVES):
        extra = [normed, query_grad] if n else []
        base = 10
        normed, query_grad, ki, vi = call(
            functools.partial(back_kernel, per, full), f"back{n}",
            [part(n)] * 3 + [local, square, states, local, gain_part(n), sums_spec, sums_spec] + [untouched] * len(extra),
            [part(n), part(n), local, local], [wide, wide, half32, half32],
            aliases={base: 0, base + 1: 1} if n else None, flops=7 * mm,
        )(queries, key_vectors, value_vectors, ag[n], intra[n][0], state[n], attended[n], gain, sums, other, *extra)
        kin.append(ki)
        vin.append(vi)
    key_grad, value_grad = None, None
    for n in range(HALVES):
        extra = [key_grad, value_grad] if n else []
        base = 9
        key_grad, value_grad = call(
            functools.partial(final_kernel, per), f"final{n}",
            [smem, smem, part(n), part(n), local, local, whole, whole, whole] + [untouched] * len(extra),
            [part(n), part(n)], [wide, wide],
            aliases={base: 0, base + 1: 1} if n else None, flops=2 * mm,
        )(block_docs, use3b, key_vectors, value_vectors, kin[n], vin[n], *gotb[n], *extra)
    return normed, query_grad, key_grad, value_grad


def solution(mesh):
    rows = P(("groups", "seq"), "head")
    in_specs = (rows, rows, rows, rows, P("head"), P(("groups", "seq")))
    out_specs = (rows, rows, rows, rows)
    seq = mesh.shape["seq"]
    short = seq == 8 and mesh.shape["head"] == 2

    def body(queries, key_vectors, value_vectors, output_grad, norm_gain, block_docs):
        one = block_docs.shape[0] == 1
        fn = block_body if short and one else general_body
        return fn(queries, key_vectors, value_vectors, output_grad, norm_gain, block_docs)

    return jax.shard_map(body, mesh=mesh, in_specs=in_specs, out_specs=out_specs, check_vma=False)
```

```python
import functools

import jax
import jax.numpy as jnp
from jax import lax
from jax.experimental import pallas as pl
from jax.experimental.pallas import tpu as pltpu
from jax.sharding import PartitionSpec as P

HEAD_DIM = 128
norm_eps = 1e-06
BF = jnp.bfloat16
F32 = jnp.float32


def spread_prefix(element, weights):
    seq_count = lax.axis_size("seq")
    flat_state = element.reshape(seq_count, -1, element.shape[-1])
    mixed = jnp.einsum(
        "ds,skc->dkc",
        weights,
        lax.all_to_all(flat_state, "seq", split_axis=0, concat_axis=0, tiled=True),
        precision=lax.Precision.HIGHEST,
    )
    returned = lax.all_to_all(mixed, "seq", split_axis=0, concat_axis=0, tiled=True)
    return returned.reshape(element.shape)


def general_body(queries, key_vectors, value_vectors, output_grad, norm_gain, block_docs):
    tokens, local_width = queries.shape
    heads_here = local_width // HEAD_DIM
    nblocks = block_docs.shape[0]
    block_len = tokens // nblocks
    shape_four = (nblocks, block_len, heads_here, HEAD_DIM)
    query_blk = queries.reshape(shape_four)
    key_blk = key_vectors.reshape(shape_four)
    value_blk = value_vectors.reshape(shape_four)
    tok_pos = lax.iota(jnp.int32, block_len)
    causal = (tok_pos[:, None] >= tok_pos[None, :])[None, None]
    scores = jnp.einsum("bthd,bshd->bhts", query_blk, key_blk, preferred_element_type=F32)
    att_weights = jnp.where(causal, scores, 0.0).astype(BF)
    intra_out = jnp.einsum("bhts,bshe->bthe", att_weights, value_blk, preferred_element_type=F32)
    block_kv = jnp.einsum("bshd,bshe->bhde", key_blk, value_blk, preferred_element_type=F32)
    position = lax.iota(jnp.int32, nblocks)
    same_doc = block_docs[:, None] == block_docs[None, :]
    earlier_mask = (same_doc & (position[None, :] < position[:, None])).astype(F32)
    later_mask = (same_doc & (position[None, :] > position[:, None])).astype(F32)
    local_in = jnp.einsum("kj,jhde->khde", earlier_mask, block_kv, precision=lax.Precision.HIGHEST)
    tail_weight = (block_docs == block_docs[-1]).astype(F32)
    tail_state = jnp.einsum("j,jhde->hde", tail_weight, block_kv, precision=lax.Precision.HIGHEST)
    seq_count = lax.axis_size("seq")
    all_docs = lax.all_gather(block_docs, "seq", axis=0, tiled=True).reshape(seq_count, nblocks)
    first_all = all_docs[:, 0]
    last_all = all_docs[:, -1]
    source_pos = lax.iota(jnp.int32, seq_count)
    forward_weights = (
        (source_pos[None, :] < source_pos[:, None]) & (last_all[None, :] == first_all[:, None])
    ).astype(F32)
    backward_weights = (
        (source_pos[None, :] > source_pos[:, None]) & (first_all[None, :] == last_all[:, None])
    ).astype(F32)
    carry_state = spread_prefix(tail_state, forward_weights)
    carry_use = block_docs == block_docs[0]
    states_in = (
        local_in + jnp.where(carry_use[:, None, None, None], carry_state[None], 0.0)
    ).astype(BF)
    inter_out = jnp.einsum("bthd,bhde->bthe", query_blk, states_in, preferred_element_type=F32)
    attended = (intra_out + inter_out).reshape(tokens, local_width)
    scaled_grad = norm_gain[None, :] * output_grad.astype(F32)
    square_sum, cross_sum = lax.psum(
        (jnp.sum(attended * attended, axis=1), jnp.sum(attended * scaled_grad, axis=1)), "head"
    )
    full_width = local_width * lax.axis_size("head")
    inverse_rms = lax.rsqrt(square_sum / full_width + norm_eps)
    normed = (attended * inverse_rms[:, None] * norm_gain[None, :]).astype(BF)
    attended_grad = (
        inverse_rms[:, None] * scaled_grad
        - attended * (inverse_rms**3 * cross_sum / full_width)[:, None]
    )
    grad_blk = attended_grad.astype(BF).reshape(shape_four)
    score_grad = jnp.einsum("bthe,bshe->bhts", grad_blk, value_blk, preferred_element_type=F32)
    grad_weights = jnp.where(causal, score_grad, 0.0).astype(BF)
    query_part = jnp.einsum("bhts,bshd->bthd", grad_weights, key_blk, preferred_element_type=F32)
    query_part = query_part + jnp.einsum(
        "bthe,bhde->bthd", grad_blk, states_in, preferred_element_type=F32
    )
    key_intra = jnp.einsum("bhts,bthd->bshd", grad_weights, query_blk, preferred_element_type=F32)
    value_intra = jnp.einsum("bhts,bthe->bshe", att_weights, grad_blk, preferred_element_type=F32)
    block_grad = jnp.einsum("bthd,bthe->bhde", query_blk, grad_blk, preferred_element_type=F32)
    grad_local = jnp.einsum(
        "kj,jhde->khde", later_mask, block_grad, precision=lax.Precision.HIGHEST
    )
    head_weight = (block_docs == block_docs[0]).astype(F32)
    head_state = jnp.einsum("j,jhde->hde", head_weight, block_grad, precision=lax.Precision.HIGHEST)
    grad_state = spread_prefix(head_state, backward_weights)
    grad_use = block_docs == block_docs[-1]
    grads_in = (
        grad_local + jnp.where(grad_use[:, None, None, None], grad_state[None], 0.0)
    ).astype(BF)
    key_part = key_intra + jnp.einsum(
        "bshe,bhde->bshd", value_blk, grads_in, preferred_element_type=F32
    )
    value_part = value_intra + jnp.einsum(
        "bshd,bhde->bshe", key_blk, grads_in, preferred_element_type=F32
    )
    flat_shape = (tokens, local_width)
    return (
        normed,
        query_part.reshape(flat_shape).astype(BF),
        key_part.reshape(flat_shape).astype(BF),
        value_part.reshape(flat_shape).astype(BF),
    )


HALVES = 2
GROUPS = 1
QUARTER_STEPS = 1
VMEM_LIMIT = 32 * 1024 * 1024


def nn(a, b):
    return lax.dot_general(a, b, (((1,), (0,)), ((), ())), preferred_element_type=F32)


def nt(a, b):
    return lax.dot_general(a, b, (((1,), (1,)), ((), ())), preferred_element_type=F32)


def tn(a, b):
    return lax.dot_general(a, b, (((0,), (0,)), ((), ())), preferred_element_type=F32)


def cols(j):
    return slice(j * HEAD_DIM, (j + 1) * HEAD_DIM)


def own_tag(doc_ref):
    return (doc_ref[0] + 1).astype(F32)


def put_head(out_ref, j, value):
    out_ref[pl.ds(j * 16, 16)] = value.reshape(16, 8, HEAD_DIM)


def put_tag(out_ref, doc_ref):
    out_ref[out_ref.shape[0] - 1] = jnp.full((8, HEAD_DIM), own_tag(doc_ref), F32)


def kv_kernel(per, doc_ref, k_ref, v_ref, out_ref):
    for j in range(per):
        put_head(out_ref, j, tn(k_ref[:, cols(j)], v_ref[:, cols(j)]))
    put_tag(out_ref, doc_ref)


def lower(n):
    return lax.broadcasted_iota(jnp.int32, (n, n), 0) >= lax.broadcasted_iota(jnp.int32, (n, n), 1)


def lower_t(n):
    return lax.broadcasted_iota(jnp.int32, (n, n), 0) <= lax.broadcasted_iota(jnp.int32, (n, n), 1)


def intra_kernel(per, q_ref, k_ref, v_ref, after_ref, out_ref):
    mask = lower(q_ref.shape[0])
    for j in range(per):
        scores = nt(q_ref[:, cols(j)], k_ref[:, cols(j)])
        att = jnp.where(mask, scores, 0.0).astype(BF)
        out_ref[:, cols(j)] = nn(att, v_ref[:, cols(j)])


def gate(doc_ref, flag_ref, r1_ref, r2_ref, r3_ref):
    own = own_tag(doc_ref)
    last = r1_ref.shape[0] - 1
    use3 = flag_ref[0]
    m1 = ((r1_ref[last] == own) & (use3 == 0)).astype(F32)
    m2 = (r2_ref[last] == own).astype(F32)
    m3 = ((r3_ref[last] == own) & (use3 == 1)).astype(F32)
    return m1, m2, m3


def gathered(j, gates, r1_ref, r2_ref, r3_ref):
    m1, m2, m3 = gates
    at = pl.ds(j * 16, 16)
    total = r2_ref[at] * m2 + r1_ref[at] * m1 + r3_ref[at] * m3
    return total.reshape(HEAD_DIM, HEAD_DIM).astype(BF)


def attend_kernel(per, last_half, doc_ref, flag_ref, q_ref, intra_ref, do_ref, gain_ref, r1_ref, r2_ref, r3_ref, *rest):
    if last_half:
        sum_in_ref, att_ref, state_ref, sum_ref, acc_ref = rest
    else:
        att_ref, state_ref, sum_ref, acc_ref = rest
    i = pl.program_id(0)

    @pl.when(i == 0)
    def _():
        if last_half:
            acc_ref[...] = sum_in_ref[...]
        else:
            acc_ref[...] = jnp.zeros_like(acc_ref)

    gates = gate(doc_ref, flag_ref, r1_ref, r2_ref, r3_ref)
    square = acc_ref[0]
    cross = acc_ref[1]
    for j in range(per):
        state = gathered(j, gates, r1_ref, r2_ref, r3_ref)
        state_ref[j] = state
        att = intra_ref[:, cols(j)] + nn(q_ref[:, cols(j)], state)
        att_ref[:, cols(j)] = att
        square = square + att * att
        cross = cross + att * (gain_ref[:, cols(j)] * do_ref[:, cols(j)].astype(F32))
    acc_ref[0] = square
    acc_ref[1] = cross

    @pl.when(i == pl.num_programs(0) - 1)
    def _():
        if last_half:
            lane = lax.broadcasted_iota(jnp.int32, square.shape, 1)
            sq = jnp.sum(square, axis=1, keepdims=True)
            cr = jnp.sum(cross, axis=1, keepdims=True)
            sum_ref[...] = jnp.where(lane == 0, sq, jnp.where(lane == 1, cr, 0.0))
        else:
            sum_ref[0] = square
            sum_ref[1] = cross


def scales(mine_ref, other_ref, width):
    total = mine_ref[...] + other_ref[...]
    inverse = lax.rsqrt(total[:, 0:1] / width + norm_eps)
    coef = inverse * inverse * inverse * total[:, 1:2] / width
    return inverse, coef


def grad_kernel(per, width, doc_ref, q_ref, att_ref, do_ref, gain_ref, mine_ref, other_ref, *rest):
    normed_ref, ag_ref, out_ref = rest[-3:]
    inverse, coef = scales(mine_ref, other_ref, width)
    for j in range(per):
        att = att_ref[:, cols(j)]
        scaled = gain_ref[:, cols(j)] * do_ref[:, cols(j)].astype(F32)
        normed_ref[:, cols(j)] = (att * inverse * gain_ref[:, cols(j)]).astype(BF)
        ag = (inverse * scaled - att * coef).astype(BF)
        ag_ref[:, cols(j)] = ag
        put_head(out_ref, j, tn(q_ref[:, cols(j)], ag))
    put_tag(out_ref, doc_ref)


def back_kernel(per, q_ref, k_ref, v_ref, ag_ref, state_ref, *rest):
    qg_ref, kin_ref, vin_ref = rest[-3:]
    mask = lower(q_ref.shape[0])
    upper = lower_t(q_ref.shape[0])
    for j in range(per):
        q = q_ref[:, cols(j)]
        k = k_ref[:, cols(j)]
        v = v_ref[:, cols(j)]
        ag = ag_ref[:, cols(j)]
        gw = jnp.where(mask, nt(ag, v), 0.0).astype(BF)
        qg_ref[:, cols(j)] = (nn(gw, k) + nt(ag, state_ref[j])).astype(BF)
        gw_t = jnp.where(upper, nt(v, ag), 0.0).astype(BF)
        kin_ref[:, cols(j)] = nn(gw_t, q)
        att_t = jnp.where(upper, nt(k, q), 0.0).astype(BF)
        vin_ref[:, cols(j)] = nn(att_t, ag)


def final_kernel(per, doc_ref, flag_ref, k_ref, v_ref, kin_ref, vin_ref, r1_ref, r2_ref, r3_ref, *rest):
    kg_ref, vg_ref = rest[-2:]
    gates = gate(doc_ref, flag_ref, r1_ref, r2_ref, r3_ref)
    for j in range(per):
        grads = gathered(j, gates, r1_ref, r2_ref, r3_ref)
        kg_ref[:, cols(j)] = (kin_ref[:, cols(j)] + nt(v_ref[:, cols(j)], grads)).astype(BF)
        vg_ref[:, cols(j)] = (vin_ref[:, cols(j)] + nn(k_ref[:, cols(j)], grads)).astype(BF)


def join_kernel(role_ref, own_ref, got_ref, after_ref, out_ref):
    last = own_ref.shape[0] - 1
    same = (own_ref[last] == got_ref[last]).astype(F32)

    @pl.when(role_ref[0] == 1)
    def _():
        out_ref[...] = got_ref[...] + own_ref[...] * same[None]
        out_ref[last] = got_ref[last]

    @pl.when(role_ref[0] == 0)
    def _():
        out_ref[...] = own_ref[...] + got_ref[...] * same[None]
        out_ref[last] = own_ref[last]


def order_kernel(x_ref, after_ref, out_ref):
    pass


def in_hbm(x):
    return pltpu.with_memory_space_constraint(x, pltpu.HBM)


def ordered(x, after, name):
    untouched = pl.BlockSpec(memory_space=pl.ANY)
    return pl.pallas_call(
        order_kernel,
        in_specs=[untouched, untouched],
        out_specs=untouched,
        out_shape=jax.ShapeDtypeStruct(x.shape, x.dtype),
        input_output_aliases={0: 0},
        name=name,
    )(x, in_hbm(after))


class Far(jax.ShapeDtypeStruct):
    pass


def call(kernel, name, in_specs, out_specs, out_shape, scratch=(), aliases=None, flops=0, steps=GROUPS):
    many = isinstance(out_shape, list)
    shapes = [
        pltpu.HBM(x.shape, x.dtype) if isinstance(x, Far) else x
        for x in (out_shape if many else [out_shape])
    ]
    return pl.pallas_call(
        kernel,
        grid=(steps,),
        in_specs=in_specs,
        out_specs=out_specs,
        out_shape=shapes if many else shapes[0],
        scratch_shapes=list(scratch),
        input_output_aliases=aliases or {},
        name=name,
        cost_estimate=pl.CostEstimate(flops=flops, transcendentals=0, bytes_accessed=4 << 20),
        compiler_params=pltpu.CompilerParams(
            dimension_semantics=("arbitrary",), vmem_limit_bytes=VMEM_LIMIT
        ),
    )


def pairs_of(seq, head, rule):
    out = []
    for s in range(seq):
        for h in range(head):
            to = rule(s, h)
            if to is not None and 0 <= to < seq:
                out.append((s * head + h, to * head + h))
    return out


def routes(seq, head, sign):
    first = pairs_of(seq, head, lambda s, h: s ^ 1 if h % 2 == 0 else s + 2 * sign)
    second = pairs_of(seq, head, lambda s, h: s + 2 * sign if h % 2 == 0 else s + sign)
    parity = 0 if sign > 0 else 1
    third = pairs_of(
        seq, head, lambda s, h: s + 2 * sign if h % 2 == 0 and s % 2 == parity else None
    )
    return first, second, third


def send(x, pairs):
    return lax.ppermute(x, ("seq", "head"), pairs)


def block_body(queries, key_vectors, value_vectors, output_grad, norm_gain, block_docs):
    tokens, width = queries.shape
    heads = width // HEAD_DIM
    seq = lax.axis_size("seq")
    head = lax.axis_size("head")
    full = width * head
    hh = heads // HALVES
    hw = hh * HEAD_DIM
    gain = norm_gain.reshape(1, width)
    odd_block = lax.axis_index("seq") % 2 == 1
    even_core = lax.axis_index("head") % 2 == 0
    smem = pl.BlockSpec(memory_space=pltpu.SMEM)
    untouched = pl.BlockSpec(memory_space=pl.ANY)
    per = hh // GROUPS
    pw = per * HEAD_DIM
    run = per * 16 + 1
    message = jax.ShapeDtypeStruct((GROUPS * run, 8, HEAD_DIM), F32)
    slabs = pl.BlockSpec((run, 8, HEAD_DIM), lambda i: (i, 0, 0))
    sums_spec = pl.BlockSpec((tokens, HEAD_DIM), lambda i: (0, 0))
    local = pl.BlockSpec((tokens, pw), lambda i: (0, i))
    states = pl.BlockSpec((per, HEAD_DIM, HEAD_DIM), lambda i: (i, 0, 0))
    acc_shape = jax.ShapeDtypeStruct((2, tokens, HEAD_DIM), F32)
    acc_spec = pl.BlockSpec((2, tokens, HEAD_DIM), lambda i: (0, 0, 0))
    wide = Far((tokens, width), BF)
    half32 = jax.ShapeDtypeStruct((tokens, hw), F32)
    far32 = Far((tokens, hw), F32)

    def part(n):
        return pl.BlockSpec((tokens, pw), lambda i: (0, i + n * GROUPS))

    def gain_part(n):
        return pl.BlockSpec((1, pw), lambda i: (0, i + n * GROUPS))

    mm = 2 * tokens * HEAD_DIM * HEAD_DIM * hh

    def role(sign):
        return (even_core & (odd_block if sign < 0 else ~odd_block)).astype(jnp.int32).reshape(1)

    def join(n, flag, own, got, after):
        return call(join_kernel, f"join{n}", [smem, slabs, slabs, untouched], slabs, message)(
            flag, own, got, after
        )

    def intra(n, after):
        return call(
            functools.partial(intra_kernel, per), f"intra{n}",
            [part(n)] * 3 + [untouched],
            local, far32, flops=4 * mm,
        )(queries, key_vectors, value_vectors, after)

    up = routes(seq, head, 1)
    flag = role(1)
    kv = [
        call(functools.partial(kv_kernel, per), f"kv{n}", [smem, part(n), part(n)], slabs, message, flops=mm)(
            block_docs, in_hbm(key_vectors), in_hbm(value_vectors)
        )
        for n in range(HALVES)
    ]
    got1 = [send(m, up[0]) for m in kv]
    intra0 = intra(0, kv[1])
    on0 = join(0, flag, kv[0], got1[0], in_hbm(intra0))
    got2a = send(on0, up[1])
    on1 = join(1, flag, kv[1], got1[1], on0)
    got2b = send(on1, up[1])
    intra1 = intra(1, on1)
    got2a = ordered(got2a, intra1, "order0")
    got3a = send(got2a, up[2])
    got3b = send(got2b, up[2])
    got = [(got1[0], got2a, got3a), (got1[1], got2b, got3b)]
    inner = [intra0, intra1]
    attended, state, sums = [], [], None
    for n in range(HALVES):
        last = n == HALVES - 1
        extra = [acc_spec] if n else []
        att, st, sums = call(
            functools.partial(attend_kernel, per, last), f"attend{n}",
            [smem, smem, part(n), local, part(n), gain_part(n), slabs, slabs, slabs] + extra,
            [local, states, sums_spec if last else acc_spec],
            [
                half32,
                Far((hh, HEAD_DIM, HEAD_DIM), BF),
                jax.ShapeDtypeStruct((tokens, HEAD_DIM), F32) if last else acc_shape,
            ],
            scratch=[pltpu.VMEM((2, tokens, HEAD_DIM), F32)], flops=mm,
        )(block_docs, flag, queries, in_hbm(inner[n]), in_hbm(output_grad), gain, *got[n], *([sums] if n else []))
        attended.append(att)
        state.append(st)
    other = lax.ppermute(sums, "head", [(c, c ^ 1) for c in range(head)])
    ag, bg, normed = [], [], None
    for n in range(HALVES):
        extra = [normed] if n else []
        normed, a, b = call(
            functools.partial(grad_kernel, per, full), f"grad{n}",
            [smem, part(n), local, part(n), gain_part(n), sums_spec, sums_spec] + [untouched] * n,
            [part(n), local, slabs], [wide, Far((tokens, hw), BF), message], aliases={7: 0} if n else None, flops=mm,
        )(block_docs, queries, attended[n], output_grad, gain, sums, other, *(in_hbm(x) for x in extra))
        ag.append(a)
        bg.append(b)

    qper = hh // 2 // QUARTER_STEPS
    qw = qper * HEAD_DIM

    def back(c, before, after):
        n, sub = divmod(c, 2)
        wide_spec = pl.BlockSpec((tokens, qw), lambda i: (0, i + c * QUARTER_STEPS))
        half_spec = pl.BlockSpec((tokens, qw), lambda i: (0, i + sub * QUARTER_STEPS))
        state_spec = pl.BlockSpec((qper, HEAD_DIM, HEAD_DIM), lambda i: (i + sub * QUARTER_STEPS, 0, 0))
        base = 6
        carried = list(before[: 3 if sub else 1]) if before else []
        return call(
            functools.partial(back_kernel, qper), f"back{c}",
            [wide_spec] * 3 + [half_spec, state_spec, untouched] + [untouched] * len(carried),
            [wide_spec, half_spec, half_spec], [wide, far32, far32],
            aliases={base + i: i for i in range(len(carried))}, flops=8 * mm // 2, steps=QUARTER_STEPS,
        )(queries, key_vectors, value_vectors, in_hbm(ag[n]),
          in_hbm(state[n]), after, *(in_hbm(x) for x in carried))

    down = routes(seq, head, -1)
    flag = role(-1)
    got1 = [send(m, down[0]) for m in bg]
    back0 = back(0, None, bg[1])
    on0 = join(0, flag, bg[0], got1[0], in_hbm(back0[0]))
    got2a = send(on0, down[1])
    back1 = back(1, back0, on0)
    on1 = join(1, flag, bg[1], got1[1], in_hbm(back1[0]))
    got2b = send(on1, down[1])
    back2 = back(2, back1, on1)
    got2a = ordered(got2a, back2[0], "order1")
    got3a = send(got2a, down[2])
    back3 = back(3, back2, got2a)
    got2b = ordered(got2b, back3[0], "order2")
    got3b = send(got2b, down[2])
    got = [(got1[0], got2a, got3a), (got1[1], got2b, got3b)]
    query_grad = back3[0]
    inside = [back1[1:3], back3[1:3]]
    key_grad, value_grad = None, None
    for n in range(HALVES):
        extra = [key_grad, value_grad] if n else []
        base = 9
        key_grad, value_grad = call(
            functools.partial(final_kernel, per), f"final{n}",
            [smem, smem, part(n), part(n), local, local, slabs, slabs, slabs] + [untouched] * len(extra),
            [part(n), part(n)], [wide, wide],
            aliases={base: 0, base + 1: 1} if n else None, flops=2 * mm,
        )(block_docs, flag, key_vectors, value_vectors, *(in_hbm(x) for x in inside[n]), *got[n], *(in_hbm(x) for x in extra))
    return normed, query_grad, key_grad, value_grad


def solution(mesh):
    rows = P(("groups", "seq"), "head")
    in_specs = (rows, rows, rows, rows, P("head"), P(("groups", "seq")))
    out_specs = (rows, rows, rows, rows)
    short = mesh.shape["seq"] == 8 and mesh.shape["head"] == 2

    def body(queries, key_vectors, value_vectors, output_grad, norm_gain, block_docs):
        one = block_docs.shape[0] == 1
        fn = block_body if short and one else general_body
        return fn(queries, key_vectors, value_vectors, output_grad, norm_gain, block_docs)

    return jax.shard_map(body, mesh=mesh, in_specs=in_specs, out_specs=out_specs, check_vma=False)
```

```python
import functools

import jax
import jax.numpy as jnp
from jax import lax
from jax.experimental import pallas as pl
from jax.experimental.pallas import tpu as pltpu
from jax.sharding import PartitionSpec as P

HEAD_DIM = 128
norm_eps = 1e-06
BF = jnp.bfloat16
F32 = jnp.float32


def spread_prefix(element, weights):
    seq_count = lax.axis_size("seq")
    flat_state = element.reshape(seq_count, -1, element.shape[-1])
    mixed = jnp.einsum(
        "ds,skc->dkc",
        weights,
        lax.all_to_all(flat_state, "seq", split_axis=0, concat_axis=0, tiled=True),
        precision=lax.Precision.HIGHEST,
    )
    returned = lax.all_to_all(mixed, "seq", split_axis=0, concat_axis=0, tiled=True)
    return returned.reshape(element.shape)


def general_body(queries, key_vectors, value_vectors, output_grad, norm_gain, block_docs):
    tokens, local_width = queries.shape
    heads_here = local_width // HEAD_DIM
    nblocks = block_docs.shape[0]
    block_len = tokens // nblocks
    shape_four = (nblocks, block_len, heads_here, HEAD_DIM)
    query_blk = queries.reshape(shape_four)
    key_blk = key_vectors.reshape(shape_four)
    value_blk = value_vectors.reshape(shape_four)
    tok_pos = lax.iota(jnp.int32, block_len)
    causal = (tok_pos[:, None] >= tok_pos[None, :])[None, None]
    scores = jnp.einsum("bthd,bshd->bhts", query_blk, key_blk, preferred_element_type=F32)
    att_weights = jnp.where(causal, scores, 0.0).astype(BF)
    intra_out = jnp.einsum("bhts,bshe->bthe", att_weights, value_blk, preferred_element_type=F32)
    block_kv = jnp.einsum("bshd,bshe->bhde", key_blk, value_blk, preferred_element_type=F32)
    position = lax.iota(jnp.int32, nblocks)
    same_doc = block_docs[:, None] == block_docs[None, :]
    earlier_mask = (same_doc & (position[None, :] < position[:, None])).astype(F32)
    later_mask = (same_doc & (position[None, :] > position[:, None])).astype(F32)
    local_in = jnp.einsum("kj,jhde->khde", earlier_mask, block_kv, precision=lax.Precision.HIGHEST)
    tail_weight = (block_docs == block_docs[-1]).astype(F32)
    tail_state = jnp.einsum("j,jhde->hde", tail_weight, block_kv, precision=lax.Precision.HIGHEST)
    seq_count = lax.axis_size("seq")
    all_docs = lax.all_gather(block_docs, "seq", axis=0, tiled=True).reshape(seq_count, nblocks)
    first_all = all_docs[:, 0]
    last_all = all_docs[:, -1]
    source_pos = lax.iota(jnp.int32, seq_count)
    forward_weights = (
        (source_pos[None, :] < source_pos[:, None]) & (last_all[None, :] == first_all[:, None])
    ).astype(F32)
    backward_weights = (
        (source_pos[None, :] > source_pos[:, None]) & (first_all[None, :] == last_all[:, None])
    ).astype(F32)
    carry_state = spread_prefix(tail_state, forward_weights)
    carry_use = block_docs == block_docs[0]
    states_in = (
        local_in + jnp.where(carry_use[:, None, None, None], carry_state[None], 0.0)
    ).astype(BF)
    inter_out = jnp.einsum("bthd,bhde->bthe", query_blk, states_in, preferred_element_type=F32)
    attended = (intra_out + inter_out).reshape(tokens, local_width)
    scaled_grad = norm_gain[None, :] * output_grad.astype(F32)
    square_sum, cross_sum = lax.psum(
        (jnp.sum(attended * attended, axis=1), jnp.sum(attended * scaled_grad, axis=1)), "head"
    )
    full_width = local_width * lax.axis_size("head")
    inverse_rms = lax.rsqrt(square_sum / full_width + norm_eps)
    normed = (attended * inverse_rms[:, None] * norm_gain[None, :]).astype(BF)
    attended_grad = (
        inverse_rms[:, None] * scaled_grad
        - attended * (inverse_rms**3 * cross_sum / full_width)[:, None]
    )
    grad_blk = attended_grad.astype(BF).reshape(shape_four)
    score_grad = jnp.einsum("bthe,bshe->bhts", grad_blk, value_blk, preferred_element_type=F32)
    grad_weights = jnp.where(causal, score_grad, 0.0).astype(BF)
    query_part = jnp.einsum("bhts,bshd->bthd", grad_weights, key_blk, preferred_element_type=F32)
    query_part = query_part + jnp.einsum(
        "bthe,bhde->bthd", grad_blk, states_in, preferred_element_type=F32
    )
    key_intra = jnp.einsum("bhts,bthd->bshd", grad_weights, query_blk, preferred_element_type=F32)
    value_intra = jnp.einsum("bhts,bthe->bshe", att_weights, grad_blk, preferred_element_type=F32)
    block_grad = jnp.einsum("bthd,bthe->bhde", query_blk, grad_blk, preferred_element_type=F32)
    grad_local = jnp.einsum(
        "kj,jhde->khde", later_mask, block_grad, precision=lax.Precision.HIGHEST
    )
    head_weight = (block_docs == block_docs[0]).astype(F32)
    head_state = jnp.einsum("j,jhde->hde", head_weight, block_grad, precision=lax.Precision.HIGHEST)
    grad_state = spread_prefix(head_state, backward_weights)
    grad_use = block_docs == block_docs[-1]
    grads_in = (
        grad_local + jnp.where(grad_use[:, None, None, None], grad_state[None], 0.0)
    ).astype(BF)
    key_part = key_intra + jnp.einsum(
        "bshe,bhde->bshd", value_blk, grads_in, preferred_element_type=F32
    )
    value_part = value_intra + jnp.einsum(
        "bshd,bhde->bshe", key_blk, grads_in, preferred_element_type=F32
    )
    flat_shape = (tokens, local_width)
    return (
        normed,
        query_part.reshape(flat_shape).astype(BF),
        key_part.reshape(flat_shape).astype(BF),
        value_part.reshape(flat_shape).astype(BF),
    )


HALVES = 2
CHUNKS = 4
VMEM_LIMIT = 16 * 1024 * 1024


def nn(a, b):
    return lax.dot_general(a, b, (((1,), (0,)), ((), ())), preferred_element_type=F32)


def nt(a, b):
    return lax.dot_general(a, b, (((1,), (1,)), ((), ())), preferred_element_type=F32)


def tn(a, b):
    return lax.dot_general(a, b, (((0,), (0,)), ((), ())), preferred_element_type=F32)


def cols(j):
    return slice(j * HEAD_DIM, (j + 1) * HEAD_DIM)


def own_tag(doc_ref):
    return (doc_ref[0] + 1).astype(F32)


def put_head(out_ref, j, value):
    out_ref[j * 16 : (j + 1) * 16] = value.reshape(16, 8, HEAD_DIM)


def put_tag(out_ref, doc_ref):
    out_ref[out_ref.shape[0] - 1] = jnp.full((8, HEAD_DIM), own_tag(doc_ref), F32)


def kv_kernel(n, hh, doc_ref, k_hbm, v_hbm, k_ref, v_ref, out_ref, k_sems, v_sems):
    step = hh // CHUNKS
    width = step * HEAD_DIM

    def copies(c):
        there = slice((n * CHUNKS + c) * width, (n * CHUNKS + c + 1) * width)
        here = slice(c * width, (c + 1) * width)
        return (
            pltpu.make_async_copy(k_hbm.at[:, there], k_ref.at[:, here], k_sems.at[c]),
            pltpu.make_async_copy(v_hbm.at[:, there], v_ref.at[:, here], v_sems.at[c]),
        )

    for c in range(CHUNKS):
        for copy in copies(c):
            copy.start()
    put_tag(out_ref, doc_ref)
    for c in range(CHUNKS):
        for copy in copies(c):
            copy.wait()
        for j in range(c * step, (c + 1) * step):
            put_head(out_ref, j, tn(k_ref[:, cols(j)], v_ref[:, cols(j)]))


def lower(n):
    return lax.broadcasted_iota(jnp.int32, (n, n), 0) >= lax.broadcasted_iota(jnp.int32, (n, n), 1)


def upper(n):
    return lax.broadcasted_iota(jnp.int32, (n, n), 0) <= lax.broadcasted_iota(jnp.int32, (n, n), 1)


def intra_kernel(n, hh, q_ref, k_ref, v_ref, after_ref, out_ref):
    mask = lower(q_ref.shape[0])
    for j in range(hh):
        scores = nt(q_ref[:, cols(n * hh + j)], k_ref[:, cols(j)])
        att = jnp.where(mask, scores, 0.0).astype(BF)
        out_ref[:, cols(j)] = nn(att, v_ref[:, cols(j)])


def near_block(parity):
    even_core = 1 - (lax.axis_index("head") & 1)
    odd_block = lax.axis_index("seq") & 1
    return even_core * (odd_block if parity else 1 - odd_block)


def gate(parity, doc_ref, r1_ref, r2_ref, r3_ref):
    own = own_tag(doc_ref)
    last = r1_ref.shape[0] - 1
    use3 = near_block(parity).astype(F32)
    m1 = (r1_ref[last] == own).astype(F32) * (1.0 - use3)
    m2 = (r2_ref[last] == own).astype(F32)
    m3 = (r3_ref[last] == own).astype(F32) * use3
    return m1, m2, m3


def gathered(j, gates, r1_ref, r2_ref, r3_ref):
    m1, m2, m3 = gates
    at = slice(j * 16, (j + 1) * 16)
    total = r2_ref[at] * m2 + r1_ref[at] * m1 + r3_ref[at] * m3
    return total.reshape(HEAD_DIM, HEAD_DIM).astype(BF)


def attend_kernel(n, hh, doc_ref, q_ref, intra_ref, do_ref, gain_ref, r1_ref, r2_ref, r3_ref, *rest):
    last_half = n == HALVES - 1
    if n:
        sum_in_ref, att_ref, state_ref, sum_ref = rest
        square = sum_in_ref[0]
        cross = sum_in_ref[1]
    else:
        att_ref, state_ref, sum_ref = rest
        square = jnp.zeros((q_ref.shape[0], HEAD_DIM), F32)
        cross = square
    gates = gate(0, doc_ref, r1_ref, r2_ref, r3_ref)
    for j in range(hh):
        at = cols(n * hh + j)
        state = gathered(j, gates, r1_ref, r2_ref, r3_ref)
        state_ref[j] = state
        att = intra_ref[:, cols(j)] + nn(q_ref[:, at], state)
        att_ref[:, cols(j)] = att
        square = square + att * att
        cross = cross + att * (gain_ref[:, at] * do_ref[:, at].astype(F32))
    if last_half:
        lane = lax.broadcasted_iota(jnp.int32, square.shape, 1)
        sq = jnp.sum(square, axis=1, keepdims=True)
        cr = jnp.sum(cross, axis=1, keepdims=True)
        sum_ref[...] = jnp.where(lane == 0, sq, jnp.where(lane == 1, cr, 0.0))
    else:
        sum_ref[0] = square
        sum_ref[1] = cross


def grad_kernel(n, hh, width, doc_ref, q_ref, att_ref, do_ref, gain_ref, mine_ref, other_ref, *rest):
    normed_ref, ag_ref, out_ref = rest[-3:]
    total = mine_ref[...] + other_ref[...]
    inverse = lax.rsqrt(total[:, 0:1] / width + norm_eps)
    coef = inverse * inverse * inverse * total[:, 1:2] / width
    for j in range(hh):
        at = cols(n * hh + j)
        att = att_ref[:, cols(j)]
        scaled = gain_ref[:, at] * do_ref[:, at].astype(F32)
        normed_ref[:, at] = (att * inverse * gain_ref[:, at]).astype(BF)
        ag = (inverse * scaled - att * coef).astype(BF)
        ag_ref[:, cols(j)] = ag
        put_head(out_ref, j, tn(q_ref[:, at], ag))
    put_tag(out_ref, doc_ref)


def back_kernel(c, hh, q_ref, k_ref, v_ref, ag_ref, state_ref, *rest):
    qg_ref, qg_sems, normed_sem = rest[-3:]
    if c == 0:
        normed_ref = rest[1]
        normed_hbm, qg_hbm, kin_ref, vin_ref = rest[-7:-3]
        normed_copy = pltpu.make_async_copy(normed_ref, normed_hbm, normed_sem)
        normed_copy.start()
    else:
        qg_hbm, kin_ref, vin_ref = rest[-6:-3]
    mask = lower(q_ref.shape[0])
    mask_t = upper(q_ref.shape[0])
    count = hh // 2
    copies = []
    for i in range(count):
        at = cols(c * count + i)
        j = (c % 2) * count + i
        q = q_ref[:, at]
        k = k_ref[:, cols(j)]
        v = v_ref[:, cols(j)]
        ag = ag_ref[:, cols(j)]
        gw = jnp.where(mask, nt(ag, v), 0.0).astype(BF)
        qg_ref[:, cols(i)] = (nn(gw, k) + nt(ag, state_ref[j])).astype(BF)
        copies.append(pltpu.make_async_copy(qg_ref.at[:, cols(i)], qg_hbm.at[:, at], qg_sems.at[i]))
        copies[-1].start()
        gw_t = jnp.where(mask_t, nt(v, ag), 0.0).astype(BF)
        kin_ref[:, cols(i)] = nn(gw_t, q)
        att_t = jnp.where(mask_t, nt(k, q), 0.0).astype(BF)
        vin_ref[:, cols(i)] = nn(att_t, ag)
    for copy in copies:
        copy.wait()
    if c == 0:
        normed_copy.wait()


def final_kernel(n, hh, doc_ref, k_ref, v_ref, kin0, kin1, vin0, vin1, r1_ref, r2_ref, r3_ref, *rest):
    kg_hbm, vg_hbm, kg_ref, vg_ref, k_sems, v_sems = rest[-6:]
    gates = gate(1, doc_ref, r1_ref, r2_ref, r3_ref)
    count = hh // 2
    step = hh // CHUNKS
    width = step * HEAD_DIM

    def copies(c):
        there = slice((n * CHUNKS + c) * width, (n * CHUNKS + c + 1) * width)
        here = slice(c * width, (c + 1) * width)
        return (
            pltpu.make_async_copy(kg_ref.at[:, here], kg_hbm.at[:, there], k_sems.at[c]),
            pltpu.make_async_copy(vg_ref.at[:, here], vg_hbm.at[:, there], v_sems.at[c]),
        )

    for c in range(CHUNKS):
        for j in range(c * step, (c + 1) * step):
            kin_ref, vin_ref = (kin0, vin0) if j < count else (kin1, vin1)
            within = cols(j % count)
            grads = gathered(j, gates, r1_ref, r2_ref, r3_ref)
            kg_ref[:, cols(j)] = (kin_ref[:, within] + nt(v_ref[:, cols(j)], grads)).astype(BF)
            vg_ref[:, cols(j)] = (vin_ref[:, within] + nn(k_ref[:, cols(j)], grads)).astype(BF)
        for copy in copies(c):
            copy.start()
    for c in range(CHUNKS):
        for copy in copies(c):
            copy.wait()


def join_kernel(parity, own_ref, got_ref, after_ref, out_ref):
    role = near_block(parity)
    last = own_ref.shape[0] - 1
    same = (own_ref[last] == got_ref[last]).astype(F32)

    @pl.when(role == 1)
    def _():
        out_ref[...] = got_ref[...] + own_ref[...] * same[None]
        out_ref[last] = got_ref[last]

    @pl.when(role == 0)
    def _():
        out_ref[...] = own_ref[...] + got_ref[...] * same[None]
        out_ref[last] = own_ref[last]


def order_kernel(x_ref, after_ref, out_ref):
    pass


VMEM, SMEM, HBM = pltpu.VMEM, pltpu.SMEM, pltpu.HBM


def call(kernel, name, ins, outs, scratch=(), aliases=None, flops=0):
    def spec(memory):
        return pl.BlockSpec(memory_space=pl.ANY if memory is HBM else memory)

    out_shape = [memory(shape, dtype) for memory, shape, dtype in outs]
    out_specs = [spec(memory) for memory, _, _ in outs]
    one = len(outs) == 1
    args = [x if m is SMEM else pltpu.with_memory_space_constraint(x, m) for m, x in ins]
    return pl.pallas_call(
        kernel,
        in_specs=[spec(m) for m, _ in ins],
        out_specs=out_specs[0] if one else out_specs,
        out_shape=out_shape[0] if one else out_shape,
        scratch_shapes=list(scratch),
        input_output_aliases=aliases or {},
        name=name,
        cost_estimate=pl.CostEstimate(flops=flops, transcendentals=0, bytes_accessed=4 << 20),
        compiler_params=pltpu.CompilerParams(vmem_limit_bytes=VMEM_LIMIT),
    )(*args)


def pairs_of(seq, head, rule):
    out = []
    for s in range(seq):
        for h in range(head):
            to = rule(s, h)
            if to is not None and 0 <= to < seq:
                out.append((s * head + h, to * head + h))
    return out


def routes(seq, head, sign):
    first = pairs_of(seq, head, lambda s, h: s ^ 1 if h % 2 == 0 else s + 2 * sign)
    second = pairs_of(seq, head, lambda s, h: s + 2 * sign if h % 2 == 0 else s + sign)
    parity = 0 if sign > 0 else 1
    third = pairs_of(
        seq, head, lambda s, h: s + 2 * sign if h % 2 == 0 and s % 2 == parity else None
    )
    return first, second, third


def send(x, pairs):
    return lax.ppermute(x, ("seq", "head"), pairs)


def block_body(queries, key_vectors, value_vectors, output_grad, norm_gain, block_docs):
    tokens, width = queries.shape
    heads = width // HEAD_DIM
    seq = lax.axis_size("seq")
    head = lax.axis_size("head")
    full = width * head
    hh = heads // HALVES
    hw = hh * HEAD_DIM
    gain = norm_gain.reshape(1, width)
    message = (VMEM, (hh * 16 + 1, 8, HEAD_DIM), F32)
    wide = (VMEM, (tokens, width), BF)
    half16 = (VMEM, (tokens, hw), BF)
    half32 = (VMEM, (tokens, hw), F32)
    quarter32 = (VMEM, (tokens, hw // 2), F32)
    sums_shape = (VMEM, (tokens, HEAD_DIM), F32)
    state_shape = (VMEM, (hh, HEAD_DIM, HEAD_DIM), BF)
    mm = 2 * tokens * HEAD_DIM * HEAD_DIM * hh
    sems = [pltpu.SemaphoreType.DMA((CHUNKS,))] * 2
    docs = (SMEM, block_docs)

    def near(*arrays):
        return [(VMEM, x) for x in arrays]

    def join(n, parity, own, got, after):
        return call(functools.partial(join_kernel, parity), f"join{n}", near(own, got, after), [message])

    def ordered(x, after, name):
        return call(order_kernel, name, near(x, after), [(VMEM, x.shape, x.dtype)], aliases={0: 0})

    def intra(n, after):
        return call(
            functools.partial(intra_kernel, n, hh), f"intra{n}",
            near(queries, keys[n], values[n], after), [half32], flops=4 * mm,
        )

    up = routes(seq, head, 1)
    keys, values, kv = zip(*(
        call(
            functools.partial(kv_kernel, n, hh), f"kv{n}",
            [docs, (HBM, key_vectors), (HBM, value_vectors)], [half16, half16, message],
            scratch=sems, flops=mm,
        )
        for n in range(HALVES)
    ))
    got1 = [send(m, up[0]) for m in kv]
    intra0 = intra(0, kv[1])
    on0 = join(0, 0, kv[0], got1[0], intra0)
    got2a = send(on0, up[1])
    on1 = join(1, 0, kv[1], got1[1], on0)
    got2b = send(on1, up[1])
    intra1 = intra(1, on1)
    got2a = ordered(got2a, intra1, "order0")
    got3a = send(got2a, up[2])
    got3b = send(got2b, up[2])
    got = [(got1[0], got2a, got3a), (got1[1], got2b, got3b)]
    inner = [intra0, intra1]
    attended, state, sums = [], [], None
    for n in range(HALVES):
        last = n == HALVES - 1
        att, st, sums = call(
            functools.partial(attend_kernel, n, hh), f"attend{n}",
            [docs] + near(queries, inner[n], output_grad, gain, *got[n], *([sums] if n else [])),
            [half32, state_shape, sums_shape if last else (VMEM, (2, tokens, HEAD_DIM), F32)],
            flops=mm,
        )
        attended.append(att)
        state.append(st)
    other = lax.ppermute(sums, "head", [(c, c ^ 1) for c in range(head)])
    ag, bg, normed = [], [], None
    for n in range(HALVES):
        normed, a, b = call(
            functools.partial(grad_kernel, n, hh, full), f"grad{n}",
            [docs] + near(queries, attended[n], output_grad, gain, sums, other, *([normed] if n else [])),
            [wide, half16, message], aliases={7: 0} if n else None, flops=mm,
        )
        ag.append(a)
        bg.append(b)

    def back(c, query_grad, after):
        n = c // 2
        ins = near(queries, keys[n], values[n], ag[n], state[n], after)
        ins += [(HBM, query_grad)] if c else near(normed)
        outs = [(HBM, (tokens, width), BF), quarter32, quarter32]
        return call(
            functools.partial(back_kernel, c, hh), f"back{c}", ins, outs if c else [outs[0]] + outs,
            scratch=[
                pltpu.VMEM((tokens, hw // 2), BF), pltpu.SemaphoreType.DMA((hh // 2,)), pltpu.SemaphoreType.DMA(())
            ],
            aliases={6: 0} if c else None, flops=7 * mm // 2,
        )

    down = routes(seq, head, -1)
    got1 = [send(m, down[0]) for m in bg]
    normed, query_grad, kin0, vin0 = back(0, None, bg[1])
    on0 = join(0, 1, bg[0], got1[0], kin0)
    got2a = send(on0, down[1])
    query_grad, kin1, vin1 = back(1, query_grad, on0)
    on1 = join(1, 1, bg[1], got1[1], kin1)
    got2b = send(on1, down[1])
    query_grad, kin2, vin2 = back(2, query_grad, on1)
    got2a = ordered(got2a, kin2, "order1")
    got3a = send(got2a, down[2])
    query_grad, kin3, vin3 = back(3, query_grad, got2a)
    got2b = ordered(got2b, kin3, "order2")
    got3b = send(got2b, down[2])
    got = [(got1[0], got2a, got3a), (got1[1], got2b, got3b)]
    inside = [(kin0, kin1, vin0, vin1), (kin2, kin3, vin2, vin3)]
    grads = None
    for n in range(HALVES):
        grads = call(
            functools.partial(final_kernel, n, hh), f"final{n}",
            [docs] + near(keys[n], values[n], *inside[n], *got[n]) + ([(HBM, x) for x in grads] if n else []),
            [(HBM, (tokens, width), BF)] * 2,
            scratch=[pltpu.VMEM((tokens, hw), BF)] * 2 + sems,
            aliases={10: 0, 11: 1} if n else None, flops=2 * mm,
        )
    return normed, query_grad, *grads


def solution(mesh):
    rows = P(("groups", "seq"), "head")
    in_specs = (rows, rows, rows, rows, P("head"), P(("groups", "seq")))
    out_specs = (rows, rows, rows, rows)
    short = mesh.shape["seq"] == 8 and mesh.shape["head"] == 2

    def body(queries, key_vectors, value_vectors, output_grad, norm_gain, block_docs):
        one = block_docs.shape[0] == 1
        fn = block_body if short and one else general_body
        return fn(queries, key_vectors, value_vectors, output_grad, norm_gain, block_docs)

    return jax.shard_map(body, mesh=mesh, in_specs=in_specs, out_specs=out_specs, check_vma=False)
```

```python
import functools
import itertools

import jax
import jax.numpy as jnp
from jax import lax
from jax.experimental import pallas as pl
from jax.experimental.pallas import tpu as pltpu
from jax.sharding import PartitionSpec as P

HEAD_DIM = 128
norm_eps = 1e-06
BF = jnp.bfloat16
F32 = jnp.float32


def spread_prefix(element, weights):
    seq_count = lax.axis_size("seq")
    flat_state = element.reshape(seq_count, -1, element.shape[-1])
    mixed = jnp.einsum(
        "ds,skc->dkc",
        weights,
        lax.all_to_all(flat_state, "seq", split_axis=0, concat_axis=0, tiled=True),
        precision=lax.Precision.HIGHEST,
    )
    returned = lax.all_to_all(mixed, "seq", split_axis=0, concat_axis=0, tiled=True)
    return returned.reshape(element.shape)


def general_body(queries, key_vectors, value_vectors, output_grad, norm_gain, block_docs):
    tokens, local_width = queries.shape
    heads_here = local_width // HEAD_DIM
    nblocks = block_docs.shape[0]
    block_len = tokens // nblocks
    shape_four = (nblocks, block_len, heads_here, HEAD_DIM)
    query_blk = queries.reshape(shape_four)
    key_blk = key_vectors.reshape(shape_four)
    value_blk = value_vectors.reshape(shape_four)
    tok_pos = lax.iota(jnp.int32, block_len)
    causal = (tok_pos[:, None] >= tok_pos[None, :])[None, None]
    scores = jnp.einsum("bthd,bshd->bhts", query_blk, key_blk, preferred_element_type=F32)
    att_weights = jnp.where(causal, scores, 0.0).astype(BF)
    intra_out = jnp.einsum("bhts,bshe->bthe", att_weights, value_blk, preferred_element_type=F32)
    block_kv = jnp.einsum("bshd,bshe->bhde", key_blk, value_blk, preferred_element_type=F32)
    position = lax.iota(jnp.int32, nblocks)
    same_doc = block_docs[:, None] == block_docs[None, :]
    earlier_mask = (same_doc & (position[None, :] < position[:, None])).astype(F32)
    later_mask = (same_doc & (position[None, :] > position[:, None])).astype(F32)
    local_in = jnp.einsum("kj,jhde->khde", earlier_mask, block_kv, precision=lax.Precision.HIGHEST)
    tail_weight = (block_docs == block_docs[-1]).astype(F32)
    tail_state = jnp.einsum("j,jhde->hde", tail_weight, block_kv, precision=lax.Precision.HIGHEST)
    seq_count = lax.axis_size("seq")
    all_docs = lax.all_gather(block_docs, "seq", axis=0, tiled=True).reshape(seq_count, nblocks)
    first_all = all_docs[:, 0]
    last_all = all_docs[:, -1]
    source_pos = lax.iota(jnp.int32, seq_count)
    forward_weights = (
        (source_pos[None, :] < source_pos[:, None]) & (last_all[None, :] == first_all[:, None])
    ).astype(F32)
    backward_weights = (
        (source_pos[None, :] > source_pos[:, None]) & (first_all[None, :] == last_all[:, None])
    ).astype(F32)
    carry_state = spread_prefix(tail_state, forward_weights)
    carry_use = block_docs == block_docs[0]
    states_in = (
        local_in + jnp.where(carry_use[:, None, None, None], carry_state[None], 0.0)
    ).astype(BF)
    inter_out = jnp.einsum("bthd,bhde->bthe", query_blk, states_in, preferred_element_type=F32)
    attended = (intra_out + inter_out).reshape(tokens, local_width)
    scaled_grad = norm_gain[None, :] * output_grad.astype(F32)
    square_sum, cross_sum = lax.psum(
        (jnp.sum(attended * attended, axis=1), jnp.sum(attended * scaled_grad, axis=1)), "head"
    )
    full_width = local_width * lax.axis_size("head")
    inverse_rms = lax.rsqrt(square_sum / full_width + norm_eps)
    normed = (attended * inverse_rms[:, None] * norm_gain[None, :]).astype(BF)
    attended_grad = (
        inverse_rms[:, None] * scaled_grad
        - attended * (inverse_rms**3 * cross_sum / full_width)[:, None]
    )
    grad_blk = attended_grad.astype(BF).reshape(shape_four)
    score_grad = jnp.einsum("bthe,bshe->bhts", grad_blk, value_blk, preferred_element_type=F32)
    grad_weights = jnp.where(causal, score_grad, 0.0).astype(BF)
    query_part = jnp.einsum("bhts,bshd->bthd", grad_weights, key_blk, preferred_element_type=F32)
    query_part = query_part + jnp.einsum(
        "bthe,bhde->bthd", grad_blk, states_in, preferred_element_type=F32
    )
    key_intra = jnp.einsum("bhts,bthd->bshd", grad_weights, query_blk, preferred_element_type=F32)
    value_intra = jnp.einsum("bhts,bthe->bshe", att_weights, grad_blk, preferred_element_type=F32)
    block_grad = jnp.einsum("bthd,bthe->bhde", query_blk, grad_blk, preferred_element_type=F32)
    grad_local = jnp.einsum(
        "kj,jhde->khde", later_mask, block_grad, precision=lax.Precision.HIGHEST
    )
    head_weight = (block_docs == block_docs[0]).astype(F32)
    head_state = jnp.einsum("j,jhde->hde", head_weight, block_grad, precision=lax.Precision.HIGHEST)
    grad_state = spread_prefix(head_state, backward_weights)
    grad_use = block_docs == block_docs[-1]
    grads_in = (
        grad_local + jnp.where(grad_use[:, None, None, None], grad_state[None], 0.0)
    ).astype(BF)
    key_part = key_intra + jnp.einsum(
        "bshe,bhde->bshd", value_blk, grads_in, preferred_element_type=F32
    )
    value_part = value_intra + jnp.einsum(
        "bshd,bhde->bshe", key_blk, grads_in, preferred_element_type=F32
    )
    flat_shape = (tokens, local_width)
    return (
        normed,
        query_part.reshape(flat_shape).astype(BF),
        key_part.reshape(flat_shape).astype(BF),
        value_part.reshape(flat_shape).astype(BF),
    )


HALVES = 2
CHUNKS = 2
VMEM_LIMIT = 16 * 1024 * 1024


def nn(a, b):
    return lax.dot_general(a, b, (((1,), (0,)), ((), ())), preferred_element_type=F32)


def nt(a, b):
    return lax.dot_general(a, b, (((1,), (1,)), ((), ())), preferred_element_type=F32)


def tn(a, b):
    return lax.dot_general(a, b, (((0,), (0,)), ((), ())), preferred_element_type=F32)


def cols(j):
    return slice(j * HEAD_DIM, (j + 1) * HEAD_DIM)


def own_tag(doc_ref):
    return (doc_ref[0] + 1).astype(F32)


def put_head(out_ref, j, value):
    out_ref[j * 16 : (j + 1) * 16] = value.reshape(16, 8, HEAD_DIM)


def put_tag(out_ref, doc_ref):
    out_ref[out_ref.shape[0] - 1] = jnp.full((8, HEAD_DIM), own_tag(doc_ref), F32)


def kv_kernel(n, hh, doc_ref, k_hbm, v_hbm, *rest):
    k_ref, v_ref, out_ref, k_sems, v_sems = rest[-5:]
    step = hh // CHUNKS
    width = step * HEAD_DIM

    def copies(c):
        there = slice((n * CHUNKS + c) * width, (n * CHUNKS + c + 1) * width)
        here = slice(c * width, (c + 1) * width)
        return (
            pltpu.make_async_copy(k_hbm.at[:, there], k_ref.at[:, here], k_sems.at[c]),
            pltpu.make_async_copy(v_hbm.at[:, there], v_ref.at[:, here], v_sems.at[c]),
        )

    for c in range(CHUNKS):
        for copy in copies(c):
            copy.start()
    put_tag(out_ref, doc_ref)
    for c in range(CHUNKS):
        for copy in copies(c):
            copy.wait()
        for j in range(c * step, (c + 1) * step):
            put_head(out_ref, j, tn(k_ref[:, cols(j)], v_ref[:, cols(j)]))


def lower(n):
    return lax.broadcasted_iota(jnp.int32, (n, n), 0) >= lax.broadcasted_iota(jnp.int32, (n, n), 1)


def upper(n):
    return lax.broadcasted_iota(jnp.int32, (n, n), 0) <= lax.broadcasted_iota(jnp.int32, (n, n), 1)


def intra_kernel(n, hh, q_ref, k_ref, v_ref, after_ref, out_ref):
    mask = lower(q_ref.shape[0])
    for j in range(hh):
        scores = nt(q_ref[:, cols(n * hh + j)], k_ref[:, cols(j)])
        att = jnp.where(mask, scores, 0.0).astype(BF)
        out_ref[:, cols(j)] = nn(att, v_ref[:, cols(j)])


def near_block(parity):
    even_core = 1 - (lax.axis_index("head") & 1)
    odd_block = lax.axis_index("seq") & 1
    return even_core * (odd_block if parity else 1 - odd_block)


def gate(parity, way, doc_ref, messages):
    own = own_tag(doc_ref)
    last = messages[0].shape[0] - 1
    gates = [(ref[last] == own).astype(F32) for ref in messages]
    if way[0] in PAIR_FIRST:
        gates[0] = gates[0] * (1.0 - near_block(parity).astype(F32))
    return gates


def gathered(j, gates, messages):
    at = slice(j * 16, (j + 1) * 16)
    total = sum(ref[at] * g for ref, g in zip(messages, gates))
    return total.reshape(HEAD_DIM, HEAD_DIM).astype(BF)


def attend_kernel(n, hh, count, doc_ref, q_ref, intra_ref, do_ref, gain_ref, *rest):
    messages, rest = rest[:count], rest[count:]
    last_half = n == HALVES - 1
    if n:
        sum_in_ref, att_ref, state_ref, sum_ref = rest
        square = sum_in_ref[0]
        cross = sum_in_ref[1]
    else:
        att_ref, state_ref, sum_ref = rest
        square = jnp.zeros((q_ref.shape[0], HEAD_DIM), F32)
        cross = square
    gates = gate(0, WAYS[n], doc_ref, messages)
    for j in range(hh):
        at = cols(n * hh + j)
        state = gathered(j, gates, messages)
        state_ref[j] = state
        att = intra_ref[:, cols(j)] + nn(q_ref[:, at], state)
        att_ref[:, cols(j)] = att
        square = square + att * att
        cross = cross + att * (gain_ref[:, at] * do_ref[:, at].astype(F32))
    if last_half:
        lane = lax.broadcasted_iota(jnp.int32, square.shape, 1)
        sq = jnp.sum(square, axis=1, keepdims=True)
        cr = jnp.sum(cross, axis=1, keepdims=True)
        sum_ref[...] = jnp.where(lane == 0, sq, jnp.where(lane == 1, cr, 0.0))
    else:
        sum_ref[0] = square
        sum_ref[1] = cross


def grad_kernel(n, hh, width, doc_ref, q_ref, att_ref, do_ref, gain_ref, mine_ref, other_ref, *rest):
    normed_ref, ag_ref, out_ref = rest[-3:]
    total = mine_ref[...] + other_ref[...]
    inverse = lax.rsqrt(total[:, 0:1] / width + norm_eps)
    coef = inverse * inverse * inverse * total[:, 1:2] / width
    for j in range(hh):
        at = cols(n * hh + j)
        att = att_ref[:, cols(j)]
        scaled = gain_ref[:, at] * do_ref[:, at].astype(F32)
        normed_ref[:, at] = (att * inverse * gain_ref[:, at]).astype(BF)
        ag = (inverse * scaled - att * coef).astype(BF)
        ag_ref[:, cols(j)] = ag
        put_head(out_ref, j, tn(q_ref[:, at], ag))
    put_tag(out_ref, doc_ref)


def back_kernel(c, hh, q_ref, k_ref, v_ref, ag_ref, state_ref, *rest):
    qg_ref, qg_sems, normed_sem = rest[-3:]
    if c == 1:
        normed_ref = rest[2]
        normed_hbm, qg_hbm, kin_ref, vin_ref = rest[-7:-3]
        normed_copy = pltpu.make_async_copy(normed_ref, normed_hbm, normed_sem)
        normed_copy.start()
    else:
        qg_hbm, kin_ref, vin_ref = rest[-6:-3]
    mask = lower(q_ref.shape[0])
    mask_t = upper(q_ref.shape[0])
    count = hh // 2
    copies = []
    for i in range(count):
        at = cols(c * count + i)
        j = (c % 2) * count + i
        q = q_ref[:, at]
        k = k_ref[:, cols(j)]
        v = v_ref[:, cols(j)]
        ag = ag_ref[:, cols(j)]
        gw = jnp.where(mask, nt(ag, v), 0.0).astype(BF)
        qg_ref[:, cols(i)] = (nn(gw, k) + nt(ag, state_ref[j])).astype(BF)
        copies.append(pltpu.make_async_copy(qg_ref.at[:, cols(i)], qg_hbm.at[:, at], qg_sems.at[i]))
        copies[-1].start()
        gw_t = jnp.where(mask_t, nt(v, ag), 0.0).astype(BF)
        kin_ref[:, cols(i)] = nn(gw_t, q)
        att_t = jnp.where(mask_t, nt(k, q), 0.0).astype(BF)
        vin_ref[:, cols(i)] = nn(att_t, ag)
    for copy in copies:
        copy.wait()
    if c == 1:
        normed_copy.wait()


def final_kernel(n, hh, count_in, doc_ref, k_ref, v_ref, kin0, kin1, vin0, vin1, *rest):
    messages, rest = rest[:count_in], rest[count_in:]
    gates = gate(1, WAYS[n], doc_ref, messages)
    count = hh // 2
    copies = []
    if n:
        kg_first, vg_first, kg_hbm, vg_hbm, kg_ref, vg_ref, sems = rest
        half = hh * HEAD_DIM
        for ref, hbm in ((kg_first, kg_hbm), (vg_first, vg_hbm)):
            copies.append(pltpu.make_async_copy(ref, hbm.at[:, :half], sems.at[len(copies)]))
            copies[-1].start()
    else:
        kg_ref, vg_ref = rest
    for j in range(hh):
        kin_ref, vin_ref = (kin0, vin0) if j < count else (kin1, vin1)
        within = cols(j % count)
        grads = gathered(j, gates, messages)
        kg_ref[:, cols(j)] = (kin_ref[:, within] + nt(v_ref[:, cols(j)], grads)).astype(BF)
        vg_ref[:, cols(j)] = (vin_ref[:, within] + nn(k_ref[:, cols(j)], grads)).astype(BF)
        if n and j % 2:
            here = slice((j - 1) * HEAD_DIM, (j + 1) * HEAD_DIM)
            there = slice(half + (j - 1) * HEAD_DIM, half + (j + 1) * HEAD_DIM)
            for ref, hbm in ((kg_ref, kg_hbm), (vg_ref, vg_hbm)):
                copies.append(pltpu.make_async_copy(ref.at[:, here], hbm.at[:, there], sems.at[len(copies)]))
                copies[-1].start()
    for copy in copies:
        copy.wait()


def add_message(base_ref, got_ref, own_ref, out_ref):
    last = own_ref.shape[0] - 1
    same = (own_ref[last] == got_ref[last]).astype(F32)
    out_ref[...] = base_ref[...] + got_ref[...] * same[None]
    out_ref[last] = own_ref[last]


def join_kernel(parity, way, own_ref, got_ref, after_ref, out_ref):
    if way[0] not in PAIR_FIRST:
        add_message(own_ref, got_ref, own_ref, out_ref)
        return
    near = near_block(parity)

    @pl.when(near == 1)
    def _():
        add_message(got_ref, own_ref, got_ref, out_ref)

    @pl.when(near == 0)
    def _():
        add_message(own_ref, got_ref, own_ref, out_ref)


def third_kernel(parity, way, own_ref, sent_ref, got_ref, after_ref, third_ref, *fourth_ref):
    if way[0] not in PAIR_FIRST:
        add_message(sent_ref, got_ref, own_ref, third_ref)
        return
    near = near_block(parity)

    @pl.when(near == 1)
    def _():
        third_ref[...] = got_ref[...]
        if fourth_ref:
            add_message(own_ref, got_ref, own_ref, fourth_ref[0])

    @pl.when(near == 0)
    def _():
        add_message(sent_ref, got_ref, own_ref, third_ref)
        if fourth_ref:
            fourth_ref[0][...] = own_ref[...]


VMEM, SMEM, HBM = pltpu.VMEM, pltpu.SMEM, pltpu.HBM


def call(kernel, name, ins, outs, scratch=(), aliases=None, flops=0):
    def spec(memory):
        return pl.BlockSpec(memory_space=pl.ANY if memory is HBM else memory)

    out_shape = [memory(shape, dtype) for memory, shape, dtype in outs]
    out_specs = [spec(memory) for memory, _, _ in outs]
    one = len(outs) == 1
    args = [x if m is SMEM else pltpu.with_memory_space_constraint(x, m) for m, x in ins]
    return pl.pallas_call(
        kernel,
        in_specs=[spec(m) for m, _ in ins],
        out_specs=out_specs[0] if one else out_specs,
        out_shape=out_shape[0] if one else out_shape,
        scratch_shapes=list(scratch),
        input_output_aliases=aliases or {},
        name=name,
        cost_estimate=pl.CostEstimate(flops=flops, transcendentals=0, bytes_accessed=4 << 20),
        compiler_params=pltpu.CompilerParams(vmem_limit_bytes=VMEM_LIMIT),
    )(*args)


def pairs_of(seq, head, sign, even_core, odd_core):
    out = []
    for t in range(seq):
        for h in range(head):
            step = (odd_core if h % 2 else even_core)(t % 2)
            if step is not None and 0 <= t + step < seq:
                source, to = (t, t + step) if sign > 0 else (seq - 1 - t, seq - 1 - t - step)
                out.append((source * head + h, to * head + h))
    return out


ROUNDS = {
    "swap": (lambda odd: -1 if odd else 1, lambda odd: 2, lambda odd: None if odd else 2),
    "first": (
        lambda odd: -1 if odd else None, lambda odd: None if odd else 2,
        lambda odd: None if odd else 2, lambda odd: None if odd else 1,
    ),
    "second": (lambda odd: None if odd else 1, lambda odd: 2 if odd else None, lambda odd: 1 if odd else None),
    "across": (lambda odd: 1 if odd else None, lambda odd: None if odd else 2, lambda odd: None if odd else 1),
    "two": (lambda odd: 2, lambda odd: 1),
}
PAIR_FIRST = ("swap", "first")
WAYS = (("first", "second"), ("swap", "two"))


def routes(seq, head, sign):
    return [
        [
            pairs_of(seq, head, sign, even or never, odd or never)
            for even, odd in itertools.zip_longest(ROUNDS[way[0]], ROUNDS[way[1]])
        ]
        for way in WAYS
    ]


def never(odd):
    return None


def send(x, pairs):
    return lax.ppermute(x, ("seq", "head"), pairs)


def block_body(queries, key_vectors, value_vectors, output_grad, norm_gain, block_docs):
    tokens, width = queries.shape
    heads = width // HEAD_DIM
    seq = lax.axis_size("seq")
    head = lax.axis_size("head")
    full = width * head
    hh = heads // HALVES
    hw = hh * HEAD_DIM
    gain = norm_gain.reshape(1, width)
    message = (VMEM, (hh * 16 + 1, 8, HEAD_DIM), F32)
    wide = (VMEM, (tokens, width), BF)
    half16 = (VMEM, (tokens, hw), BF)
    half32 = (VMEM, (tokens, hw), F32)
    quarter32 = (VMEM, (tokens, hw // 2), F32)
    sums_shape = (VMEM, (tokens, HEAD_DIM), F32)
    state_shape = (VMEM, (hh, HEAD_DIM, HEAD_DIM), BF)
    mm = 2 * tokens * HEAD_DIM * HEAD_DIM * hh
    sems = [pltpu.SemaphoreType.DMA((CHUNKS,))] * 2
    docs = (SMEM, block_docs)

    def near(*arrays):
        return [(VMEM, x) for x in arrays]

    def join(n, parity, own, got, after):
        return call(
            functools.partial(join_kernel, parity, WAYS[n]), f"second{parity}{n}", near(own, got, after), [message]
        )

    def later(n, parity, pairs, own, sent, got, after):
        out = call(
            functools.partial(third_kernel, parity, WAYS[n]), f"third{parity}{n}",
            near(own, sent, got, after), [message] * (len(pairs) - 2),
        )
        if len(pairs) == 3:
            return [send(out, pairs[2])]
        fourth = send(out[1], pairs[3])
        return [send(out[0], pairs[2]), fourth]

    def intra(n, after):
        return call(
            functools.partial(intra_kernel, n, hh), f"intra{n}",
            near(queries, keys[n], values[n], after), [half32], flops=4 * mm,
        )

    way0, way1 = routes(seq, head, 1)
    def keys_values(n, *after):
        return call(
            functools.partial(kv_kernel, n, hh), f"kv{n}",
            [docs, (HBM, key_vectors), (HBM, value_vectors)] + near(*after), [half16, half16, message],
            scratch=sems, flops=mm,
        )

    keys, values, kv = map(list, zip(keys_values(0)))
    got1 = [send(kv[0], way0[0])]
    intra0 = intra(0, kv[0])
    for out, x in zip((keys, values, kv), keys_values(1, intra0)):
        out.append(x)
    got1.append(send(kv[1], way1[0]))
    on0 = join(0, 0, kv[0], got1[0], kv[1])
    got2a = send(on0, way0[1])
    on1 = join(1, 0, kv[1], got1[1], on0)
    got2b = send(on1, way1[1])
    intra1 = intra(1, on1)
    more0 = later(0, 0, way0, kv[0], on0, got2a, intra1)
    more1 = later(1, 0, way1, kv[1], on1, got2b, on1)
    got = [(got1[0], got2a, *more0), (got1[1], got2b, *more1)]
    inner = [intra0, intra1]
    attended, state, sums = [], [], None
    for n in range(HALVES):
        last = n == HALVES - 1
        att, st, sums = call(
            functools.partial(attend_kernel, n, hh, len(got[n])), f"attend{n}",
            [docs] + near(queries, inner[n], output_grad, gain, *got[n], *([sums] if n else [])),
            [half32, state_shape, sums_shape if last else (VMEM, (2, tokens, HEAD_DIM), F32)],
            flops=mm,
        )
        attended.append(att)
        state.append(st)
    other = lax.ppermute(sums, "head", [(c, c ^ 1) for c in range(head)])
    def grad(n, normed, *after):
        return call(
            functools.partial(grad_kernel, n, hh, full), f"grad{n}",
            [docs] + near(queries, attended[n], output_grad, gain, sums, other, *([normed] if n else []), *after),
            [wide, half16, message], aliases={7: 0} if n else None, flops=mm,
        )

    def back(c, query_grad, after):
        n = c // 2
        ins = near(queries, keys[n], values[n], ag[n], state[n], after)
        ins += [(HBM, query_grad)] if c else []
        ins += near(normed) if c == 1 else []
        outs = [(HBM, (tokens, width), BF), quarter32, quarter32]
        return call(
            functools.partial(back_kernel, c, hh), f"back{c}", ins, [outs[0]] + outs if c == 1 else outs,
            scratch=[
                pltpu.VMEM((tokens, hw // 2), BF), pltpu.SemaphoreType.DMA((hh // 2,)), pltpu.SemaphoreType.DMA(())
            ],
            aliases={6: int(c == 1)} if c else None, flops=7 * mm // 2,
        )

    way0, way1 = routes(seq, head, -1)
    normed, ag0, bg0 = grad(0, None)
    ag = [ag0]
    got1 = [send(bg0, way0[0])]
    query_grad, kin0, vin0 = back(0, None, bg0)
    normed, ag1, bg1 = grad(1, normed, kin0)
    ag.append(ag1)
    bg = [bg0, bg1]
    got1.append(send(bg1, way1[0]))
    on0 = join(0, 1, bg[0], got1[0], bg1)
    got2a = send(on0, way0[1])
    normed, query_grad, kin1, vin1 = back(1, query_grad, on0)
    on1 = join(1, 1, bg[1], got1[1], kin1)
    got2b = send(on1, way1[1])
    query_grad, kin2, vin2 = back(2, query_grad, on1)
    more0 = later(0, 1, way0, bg[0], on0, got2a, kin2)
    query_grad, kin3, vin3 = back(3, query_grad, on1)
    more1 = later(1, 1, way1, bg[1], on1, got2b, kin3)
    got = [(got1[0], got2a, *more0), (got1[1], got2b, *more1)]
    inside = [(kin0, kin1, vin0, vin1), (kin2, kin3, vin2, vin3)]
    grads = []
    for n in range(HALVES):
        grads = call(
            functools.partial(final_kernel, n, hh, len(got[n])), f"final{n}",
            [docs] + near(keys[n], values[n], *inside[n], *got[n], *grads),
            [(HBM, (tokens, width), BF)] * 2 if n else [half16] * 2,
            scratch=[pltpu.VMEM((tokens, hw), BF)] * 2 + [pltpu.SemaphoreType.DMA((hh + 2,))] if n else (),
            flops=2 * mm,
        )
    return normed, query_grad, *grads


def solution(mesh):
    rows = P(("groups", "seq"), "head")
    in_specs = (rows, rows, rows, rows, P("head"), P(("groups", "seq")))
    out_specs = (rows, rows, rows, rows)
    short = mesh.shape["seq"] == 8 and mesh.shape["head"] == 2

    def body(queries, key_vectors, value_vectors, output_grad, norm_gain, block_docs):
        one = block_docs.shape[0] == 1
        fn = block_body if short and one else general_body
        return fn(queries, key_vectors, value_vectors, output_grad, norm_gain, block_docs)

    return jax.shard_map(body, mesh=mesh, in_specs=in_specs, out_specs=out_specs, check_vma=False)
```

```python
import functools
import itertools

import jax
import jax.numpy as jnp
from jax import lax
from jax.experimental import pallas as pl
from jax.experimental.pallas import tpu as pltpu
from jax.sharding import PartitionSpec as P

HEAD_DIM = 128
norm_eps = 1e-06
BF = jnp.bfloat16
F32 = jnp.float32


def spread_prefix(element, weights):
    seq_count = lax.axis_size("seq")
    flat_state = element.reshape(seq_count, -1, element.shape[-1])
    mixed = jnp.einsum(
        "ds,skc->dkc",
        weights,
        lax.all_to_all(flat_state, "seq", split_axis=0, concat_axis=0, tiled=True),
        precision=lax.Precision.HIGHEST,
    )
    returned = lax.all_to_all(mixed, "seq", split_axis=0, concat_axis=0, tiled=True)
    return returned.reshape(element.shape)


def general_body(queries, key_vectors, value_vectors, output_grad, norm_gain, block_docs):
    tokens, local_width = queries.shape
    heads_here = local_width // HEAD_DIM
    nblocks = block_docs.shape[0]
    block_len = tokens // nblocks
    shape_four = (nblocks, block_len, heads_here, HEAD_DIM)
    query_blk = queries.reshape(shape_four)
    key_blk = key_vectors.reshape(shape_four)
    value_blk = value_vectors.reshape(shape_four)
    tok_pos = lax.iota(jnp.int32, block_len)
    causal = (tok_pos[:, None] >= tok_pos[None, :])[None, None]
    scores = jnp.einsum("bthd,bshd->bhts", query_blk, key_blk, preferred_element_type=F32)
    att_weights = jnp.where(causal, scores, 0.0).astype(BF)
    intra_out = jnp.einsum("bhts,bshe->bthe", att_weights, value_blk, preferred_element_type=F32)
    block_kv = jnp.einsum("bshd,bshe->bhde", key_blk, value_blk, preferred_element_type=F32)
    position = lax.iota(jnp.int32, nblocks)
    same_doc = block_docs[:, None] == block_docs[None, :]
    earlier_mask = (same_doc & (position[None, :] < position[:, None])).astype(F32)
    later_mask = (same_doc & (position[None, :] > position[:, None])).astype(F32)
    local_in = jnp.einsum("kj,jhde->khde", earlier_mask, block_kv, precision=lax.Precision.HIGHEST)
    tail_weight = (block_docs == block_docs[-1]).astype(F32)
    tail_state = jnp.einsum("j,jhde->hde", tail_weight, block_kv, precision=lax.Precision.HIGHEST)
    seq_count = lax.axis_size("seq")
    all_docs = lax.all_gather(block_docs, "seq", axis=0, tiled=True).reshape(seq_count, nblocks)
    first_all = all_docs[:, 0]
    last_all = all_docs[:, -1]
    source_pos = lax.iota(jnp.int32, seq_count)
    forward_weights = (
        (source_pos[None, :] < source_pos[:, None]) & (last_all[None, :] == first_all[:, None])
    ).astype(F32)
    backward_weights = (
        (source_pos[None, :] > source_pos[:, None]) & (first_all[None, :] == last_all[:, None])
    ).astype(F32)
    carry_state = spread_prefix(tail_state, forward_weights)
    carry_use = block_docs == block_docs[0]
    states_in = (
        local_in + jnp.where(carry_use[:, None, None, None], carry_state[None], 0.0)
    ).astype(BF)
    inter_out = jnp.einsum("bthd,bhde->bthe", query_blk, states_in, preferred_element_type=F32)
    attended = (intra_out + inter_out).reshape(tokens, local_width)
    scaled_grad = norm_gain[None, :] * output_grad.astype(F32)
    square_sum, cross_sum = lax.psum(
        (jnp.sum(attended * attended, axis=1), jnp.sum(attended * scaled_grad, axis=1)), "head"
    )
    full_width = local_width * lax.axis_size("head")
    inverse_rms = lax.rsqrt(square_sum / full_width + norm_eps)
    normed = (attended * inverse_rms[:, None] * norm_gain[None, :]).astype(BF)
    attended_grad = (
        inverse_rms[:, None] * scaled_grad
        - attended * (inverse_rms**3 * cross_sum / full_width)[:, None]
    )
    grad_blk = attended_grad.astype(BF).reshape(shape_four)
    score_grad = jnp.einsum("bthe,bshe->bhts", grad_blk, value_blk, preferred_element_type=F32)
    grad_weights = jnp.where(causal, score_grad, 0.0).astype(BF)
    query_part = jnp.einsum("bhts,bshd->bthd", grad_weights, key_blk, preferred_element_type=F32)
    query_part = query_part + jnp.einsum(
        "bthe,bhde->bthd", grad_blk, states_in, preferred_element_type=F32
    )
    key_intra = jnp.einsum("bhts,bthd->bshd", grad_weights, query_blk, preferred_element_type=F32)
    value_intra = jnp.einsum("bhts,bthe->bshe", att_weights, grad_blk, preferred_element_type=F32)
    block_grad = jnp.einsum("bthd,bthe->bhde", query_blk, grad_blk, preferred_element_type=F32)
    grad_local = jnp.einsum(
        "kj,jhde->khde", later_mask, block_grad, precision=lax.Precision.HIGHEST
    )
    head_weight = (block_docs == block_docs[0]).astype(F32)
    head_state = jnp.einsum("j,jhde->hde", head_weight, block_grad, precision=lax.Precision.HIGHEST)
    grad_state = spread_prefix(head_state, backward_weights)
    grad_use = block_docs == block_docs[-1]
    grads_in = (
        grad_local + jnp.where(grad_use[:, None, None, None], grad_state[None], 0.0)
    ).astype(BF)
    key_part = key_intra + jnp.einsum(
        "bshe,bhde->bshd", value_blk, grads_in, preferred_element_type=F32
    )
    value_part = value_intra + jnp.einsum(
        "bshd,bhde->bshe", key_blk, grads_in, preferred_element_type=F32
    )
    flat_shape = (tokens, local_width)
    return (
        normed,
        query_part.reshape(flat_shape).astype(BF),
        key_part.reshape(flat_shape).astype(BF),
        value_part.reshape(flat_shape).astype(BF),
    )


HALVES = 2
CHUNKS = 1
VMEM_LIMIT = 16 * 1024 * 1024


def nn(a, b):
    return lax.dot_general(a, b, (((1,), (0,)), ((), ())), preferred_element_type=F32)


def nt(a, b):
    return lax.dot_general(a, b, (((1,), (1,)), ((), ())), preferred_element_type=F32)


def tn(a, b):
    return lax.dot_general(a, b, (((0,), (0,)), ((), ())), preferred_element_type=F32)


def cols(j):
    return slice(j * HEAD_DIM, (j + 1) * HEAD_DIM)


def own_tag(doc_ref):
    return (doc_ref[0] + 1).astype(F32)


def put_head(out_ref, j, value):
    out_ref[j * 16 : (j + 1) * 16] = value.reshape(16, 8, HEAD_DIM)


def put_tag(out_ref, doc_ref):
    out_ref[out_ref.shape[0] - 1] = jnp.full((8, HEAD_DIM), own_tag(doc_ref), F32)


def kv_kernel(n, hh, doc_ref, k_hbm, v_hbm, *rest):
    k_ref, v_ref, out_ref, k_sems, v_sems = rest[-5:]
    step = hh // CHUNKS
    width = step * HEAD_DIM

    def copies(c):
        there = slice((n * CHUNKS + c) * width, (n * CHUNKS + c + 1) * width)
        here = slice(c * width, (c + 1) * width)
        return (
            pltpu.make_async_copy(k_hbm.at[:, there], k_ref.at[:, here], k_sems.at[c]),
            pltpu.make_async_copy(v_hbm.at[:, there], v_ref.at[:, here], v_sems.at[c]),
        )

    for c in range(CHUNKS):
        for copy in copies(c):
            copy.start()
    put_tag(out_ref, doc_ref)
    for c in range(CHUNKS):
        for copy in copies(c):
            copy.wait()
        for j in range(c * step, (c + 1) * step):
            put_head(out_ref, j, tn(k_ref[:, cols(j)], v_ref[:, cols(j)]))


def lower(n):
    return lax.broadcasted_iota(jnp.int32, (n, n), 0) >= lax.broadcasted_iota(jnp.int32, (n, n), 1)


def upper(n):
    return lax.broadcasted_iota(jnp.int32, (n, n), 0) <= lax.broadcasted_iota(jnp.int32, (n, n), 1)


def intra_kernel(n, hh, q_ref, k_ref, v_ref, after_ref, out_ref):
    mask = lower(q_ref.shape[0])
    for j in range(hh):
        scores = nt(q_ref[:, cols(n * hh + j)], k_ref[:, cols(j)])
        att = jnp.where(mask, scores, 0.0).astype(BF)
        out_ref[:, cols(j)] = nn(att, v_ref[:, cols(j)])


def near_block(parity):
    even_core = 1 - (lax.axis_index("head") & 1)
    odd_block = lax.axis_index("seq") & 1
    return even_core * (odd_block if parity else 1 - odd_block)


def gate(parity, way, doc_ref, messages):
    own = own_tag(doc_ref)
    last = messages[0].shape[0] - 1
    gates = [(ref[last] == own).astype(F32) for ref in messages]
    if way[0] in PAIR_FIRST:
        gates[0] = gates[0] * (1.0 - near_block(parity).astype(F32))
    return gates


def gathered(j, gates, messages):
    at = slice(j * 16, (j + 1) * 16)
    total = sum(ref[at] * g for ref, g in zip(messages, gates))
    return total.reshape(HEAD_DIM, HEAD_DIM).astype(BF)


def attend_kernel(n, hh, count, doc_ref, q_ref, intra_ref, do_ref, gain_ref, *rest):
    messages, rest = rest[:count], rest[count:]
    last_half = n == HALVES - 1
    if n:
        sum_in_ref, att_ref, state_ref, sum_ref = rest
        square = sum_in_ref[0]
        cross = sum_in_ref[1]
    else:
        att_ref, state_ref, sum_ref = rest
        square = jnp.zeros((q_ref.shape[0], HEAD_DIM), F32)
        cross = square
    gates = gate(0, WAYS[n], doc_ref, messages)
    for j in range(hh):
        at = cols(n * hh + j)
        state = gathered(j, gates, messages)
        state_ref[j] = state
        att = intra_ref[:, cols(j)] + nn(q_ref[:, at], state)
        att_ref[:, cols(j)] = att
        square = square + att * att
        cross = cross + att * (gain_ref[:, at] * do_ref[:, at].astype(F32))
    if last_half:
        lane = lax.broadcasted_iota(jnp.int32, square.shape, 1)
        sq = jnp.sum(square, axis=1, keepdims=True)
        cr = jnp.sum(cross, axis=1, keepdims=True)
        sum_ref[...] = jnp.where(lane == 0, sq, jnp.where(lane == 1, cr, 0.0))
    else:
        sum_ref[0] = square
        sum_ref[1] = cross


def grad_kernel(n, hh, width, doc_ref, q_ref, att_ref, do_ref, gain_ref, mine_ref, other_ref, *rest):
    normed_ref, ag_ref, out_ref = rest[-3:]
    total = mine_ref[...] + other_ref[...]
    inverse = lax.rsqrt(total[:, 0:1] / width + norm_eps)
    coef = inverse * inverse * inverse * total[:, 1:2] / width
    for j in range(hh):
        at = cols(n * hh + j)
        att = att_ref[:, cols(j)]
        scaled = gain_ref[:, at] * do_ref[:, at].astype(F32)
        normed_ref[:, at] = (att * inverse * gain_ref[:, at]).astype(BF)
        ag = (inverse * scaled - att * coef).astype(BF)
        ag_ref[:, cols(j)] = ag
        put_head(out_ref, j, tn(q_ref[:, at], ag))
    put_tag(out_ref, doc_ref)


def back_kernel(c, hh, q_ref, k_ref, v_ref, ag_ref, state_ref, *rest):
    qg_ref, qg_sems, normed_sem = rest[-3:]
    if c == 1:
        normed_ref = rest[2]
        normed_hbm, qg_hbm, kin_ref, vin_ref = rest[-7:-3]
        normed_copy = pltpu.make_async_copy(normed_ref, normed_hbm, normed_sem)
        normed_copy.start()
    else:
        qg_hbm, kin_ref, vin_ref = rest[-6:-3]
    mask = lower(q_ref.shape[0])
    mask_t = upper(q_ref.shape[0])
    count = hh // 2
    copies = []
    for i in range(count):
        at = cols(c * count + i)
        j = (c % 2) * count + i
        q = q_ref[:, at]
        k = k_ref[:, cols(j)]
        v = v_ref[:, cols(j)]
        ag = ag_ref[:, cols(j)]
        gw = jnp.where(mask, nt(ag, v), 0.0).astype(BF)
        qg_ref[:, cols(i)] = (nn(gw, k) + nt(ag, state_ref[j])).astype(BF)
        if i == count - 1:
            there = slice(c * count * HEAD_DIM, (c + 1) * count * HEAD_DIM)
            copies.append(pltpu.make_async_copy(qg_ref, qg_hbm.at[:, there], qg_sems.at[0]))
            copies[-1].start()
        gw_t = jnp.where(mask_t, nt(v, ag), 0.0).astype(BF)
        kin_ref[:, cols(i)] = nn(gw_t, q)
        att_t = jnp.where(mask_t, nt(k, q), 0.0).astype(BF)
        vin_ref[:, cols(i)] = nn(att_t, ag)
    for copy in copies:
        copy.wait()
    if c == 1:
        normed_copy.wait()


def final_kernel(n, hh, count_in, doc_ref, k_ref, v_ref, kin0, kin1, vin0, vin1, *rest):
    messages, rest = rest[:count_in], rest[count_in:]
    gates = gate(1, WAYS[n], doc_ref, messages)
    count = hh // 2
    copies = []
    if n:
        kg_first, vg_first, kg_hbm, vg_hbm, kg_ref, vg_ref, sems = rest
        half = hh * HEAD_DIM
        for ref, hbm in ((kg_first, kg_hbm), (vg_first, vg_hbm)):
            copies.append(pltpu.make_async_copy(ref, hbm.at[:, :half], sems.at[len(copies)]))
            copies[-1].start()
    else:
        kg_ref, vg_ref = rest
    for j in range(hh):
        kin_ref, vin_ref = (kin0, vin0) if j < count else (kin1, vin1)
        within = cols(j % count)
        grads = gathered(j, gates, messages)
        kg_ref[:, cols(j)] = (kin_ref[:, within] + nt(v_ref[:, cols(j)], grads)).astype(BF)
        vg_ref[:, cols(j)] = (vin_ref[:, within] + nn(k_ref[:, cols(j)], grads)).astype(BF)
        if n and (j + 1) % count == 0:
            here = slice((j + 1 - count) * HEAD_DIM, (j + 1) * HEAD_DIM)
            there = slice(half + here.start, half + here.stop)
            for ref, hbm in ((kg_ref, kg_hbm), (vg_ref, vg_hbm)):
                copies.append(pltpu.make_async_copy(ref.at[:, here], hbm.at[:, there], sems.at[len(copies)]))
                copies[-1].start()
    for copy in copies:
        copy.wait()


def add_message(base_ref, got_ref, own_ref, out_ref):
    last = own_ref.shape[0] - 1
    same = (own_ref[last] == got_ref[last]).astype(F32)
    out_ref[...] = base_ref[...] + got_ref[...] * same[None]
    out_ref[last] = own_ref[last]


def join_kernel(parity, way, own_ref, got_ref, after_ref, out_ref):
    if way[0] not in PAIR_FIRST:
        add_message(own_ref, got_ref, own_ref, out_ref)
        return
    near = near_block(parity)

    @pl.when(near == 1)
    def _():
        add_message(got_ref, own_ref, got_ref, out_ref)

    @pl.when(near == 0)
    def _():
        add_message(own_ref, got_ref, own_ref, out_ref)


def third_kernel(parity, way, own_ref, sent_ref, got_ref, after_ref, third_ref, *fourth_ref):
    if way[0] not in PAIR_FIRST:
        add_message(sent_ref, got_ref, own_ref, third_ref)
        return
    near = near_block(parity)

    @pl.when(near == 1)
    def _():
        third_ref[...] = got_ref[...]
        if fourth_ref:
            add_message(own_ref, got_ref, own_ref, fourth_ref[0])

    @pl.when(near == 0)
    def _():
        add_message(sent_ref, got_ref, own_ref, third_ref)
        if fourth_ref:
            fourth_ref[0][...] = own_ref[...]


VMEM, SMEM, HBM = pltpu.VMEM, pltpu.SMEM, pltpu.HBM


def call(kernel, name, ins, outs, scratch=(), aliases=None, flops=0):
    def spec(memory):
        return pl.BlockSpec(memory_space=pl.ANY if memory is HBM else memory)

    out_shape = [memory(shape, dtype) for memory, shape, dtype in outs]
    out_specs = [spec(memory) for memory, _, _ in outs]
    one = len(outs) == 1
    args = [x if m is SMEM else pltpu.with_memory_space_constraint(x, m) for m, x in ins]
    return pl.pallas_call(
        kernel,
        in_specs=[spec(m) for m, _ in ins],
        out_specs=out_specs[0] if one else out_specs,
        out_shape=out_shape[0] if one else out_shape,
        scratch_shapes=list(scratch),
        input_output_aliases=aliases or {},
        name=name,
        cost_estimate=pl.CostEstimate(flops=flops, transcendentals=0, bytes_accessed=4 << 20),
        compiler_params=pltpu.CompilerParams(vmem_limit_bytes=VMEM_LIMIT),
    )(*args)


def pairs_of(seq, head, sign, even_core, odd_core):
    out = []
    for t in range(seq):
        for h in range(head):
            step = (odd_core if h % 2 else even_core)(t % 2)
            if step is not None and 0 <= t + step < seq:
                source, to = (t, t + step) if sign > 0 else (seq - 1 - t, seq - 1 - t - step)
                out.append((source * head + h, to * head + h))
    return out


ROUNDS = {
    "swap": (lambda odd: -1 if odd else 1, lambda odd: 2, lambda odd: None if odd else 2),
    "first": (
        lambda odd: -1 if odd else None, lambda odd: None if odd else 2,
        lambda odd: None if odd else 2, lambda odd: None if odd else 1,
    ),
    "second": (lambda odd: None if odd else 1, lambda odd: 2 if odd else None, lambda odd: 1 if odd else None),
    "across": (lambda odd: 1 if odd else None, lambda odd: None if odd else 2, lambda odd: None if odd else 1),
    "two": (lambda odd: 2, lambda odd: 1),
}
PAIR_FIRST = ("swap", "first")
WAYS = (("first", "second"), ("swap", "two"))


def routes(seq, head, sign):
    return [
        [
            pairs_of(seq, head, sign, even or never, odd or never)
            for even, odd in itertools.zip_longest(ROUNDS[way[0]], ROUNDS[way[1]])
        ]
        for way in WAYS
    ]


def never(odd):
    return None


def send(x, pairs):
    return lax.ppermute(x, ("seq", "head"), pairs)


def block_body(queries, key_vectors, value_vectors, output_grad, norm_gain, block_docs):
    tokens, width = queries.shape
    heads = width // HEAD_DIM
    seq = lax.axis_size("seq")
    head = lax.axis_size("head")
    full = width * head
    hh = heads // HALVES
    hw = hh * HEAD_DIM
    gain = norm_gain.reshape(1, width)
    message = (VMEM, (hh * 16 + 1, 8, HEAD_DIM), F32)
    wide = (VMEM, (tokens, width), BF)
    half16 = (VMEM, (tokens, hw), BF)
    half32 = (VMEM, (tokens, hw), F32)
    quarter32 = (VMEM, (tokens, hw // 2), F32)
    sums_shape = (VMEM, (tokens, HEAD_DIM), F32)
    state_shape = (VMEM, (hh, HEAD_DIM, HEAD_DIM), BF)
    mm = 2 * tokens * HEAD_DIM * HEAD_DIM * hh
    sems = [pltpu.SemaphoreType.DMA((CHUNKS,))] * 2
    docs = (SMEM, block_docs)

    def near(*arrays):
        return [(VMEM, x) for x in arrays]

    def join(n, parity, own, got, after):
        return call(
            functools.partial(join_kernel, parity, WAYS[n]), f"second{parity}{n}", near(own, got, after), [message]
        )

    def later(n, parity, pairs, own, sent, got, after):
        out = call(
            functools.partial(third_kernel, parity, WAYS[n]), f"third{parity}{n}",
            near(own, sent, got, after), [message] * (len(pairs) - 2),
        )
        if len(pairs) == 3:
            return [send(out, pairs[2])]
        fourth = send(out[1], pairs[3])
        return [send(out[0], pairs[2]), fourth]

    def intra(n, after):
        return call(
            functools.partial(intra_kernel, n, hh), f"intra{n}",
            near(queries, keys[n], values[n], after), [half32], flops=4 * mm,
        )

    way0, way1 = routes(seq, head, 1)
    def keys_values(n, *after):
        return call(
            functools.partial(kv_kernel, n, hh), f"kv{n}",
            [docs, (HBM, key_vectors), (HBM, value_vectors)] + near(*after), [half16, half16, message],
            scratch=sems, flops=mm,
        )

    keys, values, kv = map(list, zip(keys_values(0)))
    got1 = [send(kv[0], way0[0])]
    intra0 = intra(0, kv[0])
    for out, x in zip((keys, values, kv), keys_values(1, intra0)):
        out.append(x)
    got1.append(send(kv[1], way1[0]))
    on0 = join(0, 0, kv[0], got1[0], kv[1])
    got2a = send(on0, way0[1])
    on1 = join(1, 0, kv[1], got1[1], on0)
    got2b = send(on1, way1[1])
    intra1 = intra(1, on1)
    more0 = later(0, 0, way0, kv[0], on0, got2a, intra1)
    more1 = later(1, 0, way1, kv[1], on1, got2b, on1)
    got = [(got1[0], got2a, *more0), (got1[1], got2b, *more1)]
    inner = [intra0, intra1]
    attended, state, sums = [], [], None
    for n in range(HALVES):
        last = n == HALVES - 1
        att, st, sums = call(
            functools.partial(attend_kernel, n, hh, len(got[n])), f"attend{n}",
            [docs] + near(queries, inner[n], output_grad, gain, *got[n], *([sums] if n else [])),
            [half32, state_shape, sums_shape if last else (VMEM, (2, tokens, HEAD_DIM), F32)],
            flops=mm,
        )
        attended.append(att)
        state.append(st)
    other = lax.ppermute(sums, "head", [(c, c ^ 1) for c in range(head)])
    def grad(n, normed, *after):
        return call(
            functools.partial(grad_kernel, n, hh, full), f"grad{n}",
            [docs] + near(queries, attended[n], output_grad, gain, sums, other, *([normed] if n else []), *after),
            [wide, half16, message], aliases={7: 0} if n else None, flops=mm,
        )

    def back(c, query_grad, after):
        n = c // 2
        ins = near(queries, keys[n], values[n], ag[n], state[n], after)
        ins += [(HBM, query_grad)] if c else []
        ins += near(normed) if c == 1 else []
        outs = [(HBM, (tokens, width), BF), quarter32, quarter32]
        return call(
            functools.partial(back_kernel, c, hh), f"back{c}", ins, [outs[0]] + outs if c == 1 else outs,
            scratch=[
                pltpu.VMEM((tokens, hw // 2), BF), pltpu.SemaphoreType.DMA((hh // 2,)), pltpu.SemaphoreType.DMA(())
            ],
            aliases={6: int(c == 1)} if c else None, flops=7 * mm // 2,
        )

    way0, way1 = routes(seq, head, -1)
    normed, ag0, bg0 = grad(0, None)
    ag = [ag0]
    got1 = [send(bg0, way0[0])]
    query_grad, kin0, vin0 = back(0, None, bg0)
    normed, ag1, bg1 = grad(1, normed, kin0)
    ag.append(ag1)
    bg = [bg0, bg1]
    got1.append(send(bg1, way1[0]))
    on0 = join(0, 1, bg[0], got1[0], bg1)
    got2a = send(on0, way0[1])
    normed, query_grad, kin1, vin1 = back(1, query_grad, on0)
    on1 = join(1, 1, bg[1], got1[1], kin1)
    got2b = send(on1, way1[1])
    query_grad, kin2, vin2 = back(2, query_grad, on1)
    more0 = later(0, 1, way0, bg[0], on0, got2a, kin2)
    more1 = later(1, 1, way1, bg[1], on1, got2b, on1)
    query_grad, kin3, vin3 = back(3, query_grad, got2b)
    got = [(got1[0], got2a, *more0), (got1[1], got2b, *more1)]
    inside = [(kin0, kin1, vin0, vin1), (kin2, kin3, vin2, vin3)]
    grads = []
    for n in range(HALVES):
        grads = call(
            functools.partial(final_kernel, n, hh, len(got[n])), f"final{n}",
            [docs] + near(keys[n], values[n], *inside[n], *got[n], *grads),
            [(HBM, (tokens, width), BF)] * 2 if n else [half16] * 2,
            scratch=[pltpu.VMEM((tokens, hw), BF)] * 2 + [pltpu.SemaphoreType.DMA((hh + 2,))] if n else (),
            flops=2 * mm,
        )
    return normed, query_grad, *grads


def solution(mesh):
    rows = P(("groups", "seq"), "head")
    in_specs = (rows, rows, rows, rows, P("head"), P(("groups", "seq")))
    out_specs = (rows, rows, rows, rows)
    short = mesh.shape["seq"] == 8 and mesh.shape["head"] == 2

    def body(queries, key_vectors, value_vectors, output_grad, norm_gain, block_docs):
        one = block_docs.shape[0] == 1
        fn = block_body if short and one else general_body
        return fn(queries, key_vectors, value_vectors, output_grad, norm_gain, block_docs)

    return jax.shard_map(body, mesh=mesh, in_specs=in_specs, out_specs=out_specs, check_vma=False)
```

```python
import functools
import itertools

import jax
import jax.numpy as jnp
from jax import lax
from jax.experimental import pallas as pl
from jax.experimental.pallas import tpu as pltpu
from jax.sharding import PartitionSpec as P

HEAD_DIM = 128
norm_eps = 1e-06
BF = jnp.bfloat16
F32 = jnp.float32


def spread_prefix(element, weights):
    seq_count = lax.axis_size("seq")
    flat_state = element.reshape(seq_count, -1, element.shape[-1])
    mixed = jnp.einsum(
        "ds,skc->dkc",
        weights,
        lax.all_to_all(flat_state, "seq", split_axis=0, concat_axis=0, tiled=True),
        precision=lax.Precision.HIGHEST,
    )
    returned = lax.all_to_all(mixed, "seq", split_axis=0, concat_axis=0, tiled=True)
    return returned.reshape(element.shape)


def general_body(queries, key_vectors, value_vectors, output_grad, norm_gain, block_docs):
    tokens, local_width = queries.shape
    heads_here = local_width // HEAD_DIM
    nblocks = block_docs.shape[0]
    block_len = tokens // nblocks
    shape_four = (nblocks, block_len, heads_here, HEAD_DIM)
    query_blk = queries.reshape(shape_four)
    key_blk = key_vectors.reshape(shape_four)
    value_blk = value_vectors.reshape(shape_four)
    tok_pos = lax.iota(jnp.int32, block_len)
    causal = (tok_pos[:, None] >= tok_pos[None, :])[None, None]
    scores = jnp.einsum("bthd,bshd->bhts", query_blk, key_blk, preferred_element_type=F32)
    att_weights = jnp.where(causal, scores, 0.0).astype(BF)
    intra_out = jnp.einsum("bhts,bshe->bthe", att_weights, value_blk, preferred_element_type=F32)
    block_kv = jnp.einsum("bshd,bshe->bhde", key_blk, value_blk, preferred_element_type=F32)
    position = lax.iota(jnp.int32, nblocks)
    same_doc = block_docs[:, None] == block_docs[None, :]
    earlier_mask = (same_doc & (position[None, :] < position[:, None])).astype(F32)
    later_mask = (same_doc & (position[None, :] > position[:, None])).astype(F32)
    local_in = jnp.einsum("kj,jhde->khde", earlier_mask, block_kv, precision=lax.Precision.HIGHEST)
    tail_weight = (block_docs == block_docs[-1]).astype(F32)
    tail_state = jnp.einsum("j,jhde->hde", tail_weight, block_kv, precision=lax.Precision.HIGHEST)
    seq_count = lax.axis_size("seq")
    all_docs = lax.all_gather(block_docs, "seq", axis=0, tiled=True).reshape(seq_count, nblocks)
    first_all = all_docs[:, 0]
    last_all = all_docs[:, -1]
    source_pos = lax.iota(jnp.int32, seq_count)
    forward_weights = (
        (source_pos[None, :] < source_pos[:, None]) & (last_all[None, :] == first_all[:, None])
    ).astype(F32)
    backward_weights = (
        (source_pos[None, :] > source_pos[:, None]) & (first_all[None, :] == last_all[:, None])
    ).astype(F32)
    carry_state = spread_prefix(tail_state, forward_weights)
    carry_use = block_docs == block_docs[0]
    states_in = (
        local_in + jnp.where(carry_use[:, None, None, None], carry_state[None], 0.0)
    ).astype(BF)
    inter_out = jnp.einsum("bthd,bhde->bthe", query_blk, states_in, preferred_element_type=F32)
    attended = (intra_out + inter_out).reshape(tokens, local_width)
    scaled_grad = norm_gain[None, :] * output_grad.astype(F32)
    square_sum, cross_sum = lax.psum(
        (jnp.sum(attended * attended, axis=1), jnp.sum(attended * scaled_grad, axis=1)), "head"
    )
    full_width = local_width * lax.axis_size("head")
    inverse_rms = lax.rsqrt(square_sum / full_width + norm_eps)
    normed = (attended * inverse_rms[:, None] * norm_gain[None, :]).astype(BF)
    attended_grad = (
        inverse_rms[:, None] * scaled_grad
        - attended * (inverse_rms**3 * cross_sum / full_width)[:, None]
    )
    grad_blk = attended_grad.astype(BF).reshape(shape_four)
    score_grad = jnp.einsum("bthe,bshe->bhts", grad_blk, value_blk, preferred_element_type=F32)
    grad_weights = jnp.where(causal, score_grad, 0.0).astype(BF)
    query_part = jnp.einsum("bhts,bshd->bthd", grad_weights, key_blk, preferred_element_type=F32)
    query_part = query_part + jnp.einsum(
        "bthe,bhde->bthd", grad_blk, states_in, preferred_element_type=F32
    )
    key_intra = jnp.einsum("bhts,bthd->bshd", grad_weights, query_blk, preferred_element_type=F32)
    value_intra = jnp.einsum("bhts,bthe->bshe", att_weights, grad_blk, preferred_element_type=F32)
    block_grad = jnp.einsum("bthd,bthe->bhde", query_blk, grad_blk, preferred_element_type=F32)
    grad_local = jnp.einsum(
        "kj,jhde->khde", later_mask, block_grad, precision=lax.Precision.HIGHEST
    )
    head_weight = (block_docs == block_docs[0]).astype(F32)
    head_state = jnp.einsum("j,jhde->hde", head_weight, block_grad, precision=lax.Precision.HIGHEST)
    grad_state = spread_prefix(head_state, backward_weights)
    grad_use = block_docs == block_docs[-1]
    grads_in = (
        grad_local + jnp.where(grad_use[:, None, None, None], grad_state[None], 0.0)
    ).astype(BF)
    key_part = key_intra + jnp.einsum(
        "bshe,bhde->bshd", value_blk, grads_in, preferred_element_type=F32
    )
    value_part = value_intra + jnp.einsum(
        "bshd,bhde->bshe", key_blk, grads_in, preferred_element_type=F32
    )
    flat_shape = (tokens, local_width)
    return (
        normed,
        query_part.reshape(flat_shape).astype(BF),
        key_part.reshape(flat_shape).astype(BF),
        value_part.reshape(flat_shape).astype(BF),
    )


HALVES = 2
CHUNKS = 1
VMEM_LIMIT = 16 * 1024 * 1024


def nn(a, b):
    return lax.dot_general(a, b, (((1,), (0,)), ((), ())), preferred_element_type=F32)


def nt(a, b):
    return lax.dot_general(a, b, (((1,), (1,)), ((), ())), preferred_element_type=F32)


def tn(a, b):
    return lax.dot_general(a, b, (((0,), (0,)), ((), ())), preferred_element_type=F32)


def cols(j):
    return slice(j * HEAD_DIM, (j + 1) * HEAD_DIM)


def own_tag(doc_ref):
    return (doc_ref[0] + 1).astype(F32)


def put_head(out_ref, j, value):
    out_ref[j * 16 : (j + 1) * 16] = value.reshape(16, 8, HEAD_DIM)


def put_tag(out_ref, doc_ref):
    out_ref[out_ref.shape[0] - 1] = jnp.full((8, HEAD_DIM), own_tag(doc_ref), F32)


def kv_kernel(n, hh, doc_ref, k_hbm, v_hbm, *rest):
    k_ref, v_ref, out_ref, k_sems, v_sems = rest[-5:]
    step = hh // CHUNKS
    width = step * HEAD_DIM

    def copies(c):
        there = slice((n * CHUNKS + c) * width, (n * CHUNKS + c + 1) * width)
        here = slice(c * width, (c + 1) * width)
        return (
            pltpu.make_async_copy(k_hbm.at[:, there], k_ref.at[:, here], k_sems.at[c]),
            pltpu.make_async_copy(v_hbm.at[:, there], v_ref.at[:, here], v_sems.at[c]),
        )

    for c in range(CHUNKS):
        for copy in copies(c):
            copy.start()
    put_tag(out_ref, doc_ref)
    for c in range(CHUNKS):
        for copy in copies(c):
            copy.wait()
        for j in range(c * step, (c + 1) * step):
            put_head(out_ref, j, tn(k_ref[:, cols(j)], v_ref[:, cols(j)]))


def lower(n):
    return lax.broadcasted_iota(jnp.int32, (n, n), 0) >= lax.broadcasted_iota(jnp.int32, (n, n), 1)


def upper(n):
    return lax.broadcasted_iota(jnp.int32, (n, n), 0) <= lax.broadcasted_iota(jnp.int32, (n, n), 1)


def intra_kernel(n, hh, q_ref, k_ref, v_ref, after_ref, out_ref):
    mask = lower(q_ref.shape[0])
    for j in range(hh):
        scores = nt(q_ref[:, cols(n * hh + j)], k_ref[:, cols(j)])
        att = jnp.where(mask, scores, 0.0).astype(BF)
        out_ref[:, cols(j)] = nn(att, v_ref[:, cols(j)])


def near_block(parity):
    even_core = 1 - (lax.axis_index("head") & 1)
    odd_block = lax.axis_index("seq") & 1
    return even_core * (odd_block if parity else 1 - odd_block)


def gate(parity, way, doc_ref, messages):
    own = own_tag(doc_ref)
    last = messages[0].shape[0] - 1
    gates = [(ref[last] == own).astype(F32) for ref in messages]
    if way[0] in PAIR_FIRST:
        gates[0] = gates[0] * (1.0 - near_block(parity).astype(F32))
    return gates


def gathered(j, gates, messages):
    at = slice(j * 16, (j + 1) * 16)
    total = sum(ref[at] * g for ref, g in zip(messages, gates))
    return total.reshape(HEAD_DIM, HEAD_DIM).astype(BF)


def attend_kernel(n, hh, count, doc_ref, q_ref, intra_ref, do_ref, gain_ref, *rest):
    messages, rest = rest[:count], rest[count:]
    last_half = n == HALVES - 1
    if n:
        sum_in_ref, att_ref, state_ref, sum_ref = rest
        square = sum_in_ref[0]
        cross = sum_in_ref[1]
    else:
        att_ref, state_ref, sum_ref = rest
        square = jnp.zeros((q_ref.shape[0], HEAD_DIM), F32)
        cross = square
    gates = gate(0, WAYS[n], doc_ref, messages)
    for j in range(hh):
        at = cols(n * hh + j)
        state = gathered(j, gates, messages)
        state_ref[j] = state
        att = intra_ref[:, cols(j)] + nn(q_ref[:, at], state)
        att_ref[:, cols(j)] = att
        square = square + att * att
        cross = cross + att * (gain_ref[:, at] * do_ref[:, at].astype(F32))
    if last_half:
        lane = lax.broadcasted_iota(jnp.int32, square.shape, 1)
        sq = jnp.sum(square, axis=1, keepdims=True)
        cr = jnp.sum(cross, axis=1, keepdims=True)
        sum_ref[...] = jnp.where(lane == 0, sq, jnp.where(lane == 1, cr, 0.0))
    else:
        sum_ref[0] = square
        sum_ref[1] = cross


def grad_kernel(n, hh, width, doc_ref, q_ref, att_ref, do_ref, gain_ref, mine_ref, other_ref, *rest):
    ag_ref, out_ref = rest[-2:]
    total = mine_ref[...] + other_ref[...]
    inverse = lax.rsqrt(total[:, 0:1] / width + norm_eps)
    coef = inverse * inverse * inverse * total[:, 1:2] / width
    for j in range(hh):
        at = cols(n * hh + j)
        att = att_ref[:, cols(j)]
        scaled = gain_ref[:, at] * do_ref[:, at].astype(F32)
        ag = (inverse * scaled - att * coef).astype(BF)
        ag_ref[:, cols(j)] = ag
        put_head(out_ref, j, tn(q_ref[:, at], ag))
    put_tag(out_ref, doc_ref)


def back_kernel(c, hh, width, q_ref, k_ref, v_ref, ag_ref, state_ref, *rest):
    qg_ref, qg_sems, normed_ref, normed_sem = rest[-4:]
    if c == 1:
        first_ref, second_ref, gain_ref, mine_ref, other_ref = rest[2:7]
        normed_hbm, qg_hbm, kin_ref, vin_ref = rest[-8:-4]
        total = mine_ref[...] + other_ref[...]
        inverse = lax.rsqrt(total[:, 0:1] / width + norm_eps)
        half = first_ref.shape[1]
        normed_ref[:, :half] = (first_ref[...] * inverse * gain_ref[:, :half]).astype(BF)
        normed_ref[:, half:] = (second_ref[...] * inverse * gain_ref[:, half:]).astype(BF)
        normed_copy = pltpu.make_async_copy(normed_ref, normed_hbm, normed_sem)
        normed_copy.start()
    else:
        qg_hbm, kin_ref, vin_ref = rest[-7:-4]
    mask = lower(q_ref.shape[0])
    mask_t = upper(q_ref.shape[0])
    count = hh // 2
    copies = []
    for i in range(count):
        at = cols(c * count + i)
        j = (c % 2) * count + i
        q = q_ref[:, at]
        k = k_ref[:, cols(j)]
        v = v_ref[:, cols(j)]
        ag = ag_ref[:, cols(j)]
        gw = jnp.where(mask, nt(ag, v), 0.0).astype(BF)
        qg_ref[:, cols(i)] = (nn(gw, k) + nt(ag, state_ref[j])).astype(BF)
        if i == count - 1:
            there = slice(c * count * HEAD_DIM, (c + 1) * count * HEAD_DIM)
            copies.append(pltpu.make_async_copy(qg_ref, qg_hbm.at[:, there], qg_sems.at[0]))
            copies[-1].start()
        gw_t = jnp.where(mask_t, nt(v, ag), 0.0).astype(BF)
        kin_ref[:, cols(i)] = nn(gw_t, q)
        att_t = jnp.where(mask_t, nt(k, q), 0.0).astype(BF)
        vin_ref[:, cols(i)] = nn(att_t, ag)
    for copy in copies:
        copy.wait()
    if c == 1:
        normed_copy.wait()


def final_kernel(n, hh, count_in, doc_ref, k_ref, v_ref, kin0, kin1, vin0, vin1, *rest):
    messages, rest = rest[:count_in], rest[count_in:]
    gates = gate(1, WAYS[n], doc_ref, messages)
    count = hh // 2
    copies = []
    if n:
        kg_first, vg_first, kg_hbm, vg_hbm, kg_ref, vg_ref, sems = rest
        half = hh * HEAD_DIM
        for ref, hbm in ((kg_first, kg_hbm), (vg_first, vg_hbm)):
            copies.append(pltpu.make_async_copy(ref, hbm.at[:, :half], sems.at[len(copies)]))
            copies[-1].start()
    else:
        kg_ref, vg_ref = rest
    for j in range(hh):
        kin_ref, vin_ref = (kin0, vin0) if j < count else (kin1, vin1)
        within = cols(j % count)
        grads = gathered(j, gates, messages)
        kg_ref[:, cols(j)] = (kin_ref[:, within] + nt(v_ref[:, cols(j)], grads)).astype(BF)
        vg_ref[:, cols(j)] = (vin_ref[:, within] + nn(k_ref[:, cols(j)], grads)).astype(BF)
        if n and (j + 1) % count == 0:
            here = slice((j + 1 - count) * HEAD_DIM, (j + 1) * HEAD_DIM)
            there = slice(half + here.start, half + here.stop)
            for ref, hbm in ((kg_ref, kg_hbm), (vg_ref, vg_hbm)):
                copies.append(pltpu.make_async_copy(ref.at[:, here], hbm.at[:, there], sems.at[len(copies)]))
                copies[-1].start()
    for copy in copies:
        copy.wait()


def add_message(base_ref, got_ref, own_ref, out_ref):
    last = own_ref.shape[0] - 1
    same = (own_ref[last] == got_ref[last]).astype(F32)
    out_ref[...] = base_ref[...] + got_ref[...] * same[None]
    out_ref[last] = own_ref[last]


def join_kernel(parity, way, own_ref, got_ref, after_ref, out_ref):
    if way[0] not in PAIR_FIRST:
        add_message(own_ref, got_ref, own_ref, out_ref)
        return
    near = near_block(parity)

    @pl.when(near == 1)
    def _():
        add_message(got_ref, own_ref, got_ref, out_ref)

    @pl.when(near == 0)
    def _():
        add_message(own_ref, got_ref, own_ref, out_ref)


def third_kernel(parity, way, own_ref, sent_ref, got_ref, after_ref, third_ref, *fourth_ref):
    if way[0] not in PAIR_FIRST:
        add_message(sent_ref, got_ref, own_ref, third_ref)
        return
    near = near_block(parity)

    @pl.when(near == 1)
    def _():
        third_ref[...] = got_ref[...]
        if fourth_ref:
            add_message(own_ref, got_ref, own_ref, fourth_ref[0])

    @pl.when(near == 0)
    def _():
        add_message(sent_ref, got_ref, own_ref, third_ref)
        if fourth_ref:
            fourth_ref[0][...] = own_ref[...]


VMEM, SMEM, HBM = pltpu.VMEM, pltpu.SMEM, pltpu.HBM


def call(kernel, name, ins, outs, scratch=(), aliases=None, flops=0):
    def spec(memory):
        return pl.BlockSpec(memory_space=pl.ANY if memory is HBM else memory)

    out_shape = [memory(shape, dtype) for memory, shape, dtype in outs]
    out_specs = [spec(memory) for memory, _, _ in outs]
    one = len(outs) == 1
    args = [x if m is SMEM else pltpu.with_memory_space_constraint(x, m) for m, x in ins]
    return pl.pallas_call(
        kernel,
        in_specs=[spec(m) for m, _ in ins],
        out_specs=out_specs[0] if one else out_specs,
        out_shape=out_shape[0] if one else out_shape,
        scratch_shapes=list(scratch),
        input_output_aliases=aliases or {},
        name=name,
        cost_estimate=pl.CostEstimate(flops=flops, transcendentals=0, bytes_accessed=4 << 20),
        compiler_params=pltpu.CompilerParams(vmem_limit_bytes=VMEM_LIMIT),
    )(*args)


def pairs_of(seq, head, sign, even_core, odd_core):
    out = []
    for t in range(seq):
        for h in range(head):
            step = (odd_core if h % 2 else even_core)(t % 2)
            if step is not None and 0 <= t + step < seq:
                source, to = (t, t + step) if sign > 0 else (seq - 1 - t, seq - 1 - t - step)
                out.append((source * head + h, to * head + h))
    return out


ROUNDS = {
    "swap": (lambda odd: -1 if odd else 1, lambda odd: 2, lambda odd: None if odd else 2),
    "first": (
        lambda odd: -1 if odd else None, lambda odd: None if odd else 2,
        lambda odd: None if odd else 2, lambda odd: None if odd else 1,
    ),
    "second": (lambda odd: None if odd else 1, lambda odd: 2 if odd else None, lambda odd: 1 if odd else None),
    "across": (lambda odd: 1 if odd else None, lambda odd: None if odd else 2, lambda odd: None if odd else 1),
    "two": (lambda odd: 2, lambda odd: 1),
}
PAIR_FIRST = ("swap", "first")
WAYS = (("first", "second"), ("swap", "two"))


def routes(seq, head, sign):
    return [
        [
            pairs_of(seq, head, sign, even or never, odd or never)
            for even, odd in itertools.zip_longest(ROUNDS[way[0]], ROUNDS[way[1]])
        ]
        for way in WAYS
    ]


def never(odd):
    return None


def send(x, pairs):
    return lax.ppermute(x, ("seq", "head"), pairs)


def block_body(queries, key_vectors, value_vectors, output_grad, norm_gain, block_docs):
    tokens, width = queries.shape
    heads = width // HEAD_DIM
    seq = lax.axis_size("seq")
    head = lax.axis_size("head")
    full = width * head
    hh = heads // HALVES
    hw = hh * HEAD_DIM
    gain = norm_gain.reshape(1, width)
    message = (VMEM, (hh * 16 + 1, 8, HEAD_DIM), F32)
    wide = (VMEM, (tokens, width), BF)
    half16 = (VMEM, (tokens, hw), BF)
    half32 = (VMEM, (tokens, hw), F32)
    quarter32 = (VMEM, (tokens, hw // 2), F32)
    sums_shape = (VMEM, (tokens, HEAD_DIM), F32)
    state_shape = (VMEM, (hh, HEAD_DIM, HEAD_DIM), BF)
    mm = 2 * tokens * HEAD_DIM * HEAD_DIM * hh
    sems = [pltpu.SemaphoreType.DMA((CHUNKS,))] * 2
    docs = (SMEM, block_docs)

    def near(*arrays):
        return [(VMEM, x) for x in arrays]

    def join(n, parity, own, got, after):
        return call(
            functools.partial(join_kernel, parity, WAYS[n]), f"second{parity}{n}", near(own, got, after), [message]
        )

    def later(n, parity, pairs, own, sent, got, after):
        out = call(
            functools.partial(third_kernel, parity, WAYS[n]), f"third{parity}{n}",
            near(own, sent, got, after), [message] * (len(pairs) - 2),
        )
        if len(pairs) == 3:
            return [send(out, pairs[2])]
        fourth = send(out[1], pairs[3])
        return [send(out[0], pairs[2]), fourth]

    def intra(n, after):
        return call(
            functools.partial(intra_kernel, n, hh), f"intra{n}",
            near(queries, keys[n], values[n], after), [half32], flops=4 * mm,
        )

    way0, way1 = routes(seq, head, 1)
    def keys_values(n, *after):
        return call(
            functools.partial(kv_kernel, n, hh), f"kv{n}",
            [docs, (HBM, key_vectors), (HBM, value_vectors)] + near(*after), [half16, half16, message],
            scratch=sems, flops=mm,
        )

    keys, values, kv = map(list, zip(keys_values(0)))
    got1 = [send(kv[0], way0[0])]
    intra0 = intra(0, kv[0])
    for out, x in zip((keys, values, kv), keys_values(1, intra0)):
        out.append(x)
    got1.append(send(kv[1], way1[0]))
    on0 = join(0, 0, kv[0], got1[0], kv[1])
    got2a = send(on0, way0[1])
    on1 = join(1, 0, kv[1], got1[1], on0)
    got2b = send(on1, way1[1])
    intra1 = intra(1, on1)
    more0 = later(0, 0, way0, kv[0], on0, got2a, intra1)
    more1 = later(1, 0, way1, kv[1], on1, got2b, on1)
    got = [(got1[0], got2a, *more0), (got1[1], got2b, *more1)]
    inner = [intra0, intra1]
    attended, state, sums = [], [], None
    for n in range(HALVES):
        last = n == HALVES - 1
        att, st, sums = call(
            functools.partial(attend_kernel, n, hh, len(got[n])), f"attend{n}",
            [docs] + near(queries, inner[n], output_grad, gain, *got[n], *([sums] if n else [])),
            [half32, state_shape, sums_shape if last else (VMEM, (2, tokens, HEAD_DIM), F32)],
            flops=mm,
        )
        attended.append(att)
        state.append(st)
    other = lax.ppermute(sums, "head", [(c, c ^ 1) for c in range(head)])
    def grad(n, *after):
        return call(
            functools.partial(grad_kernel, n, hh, full), f"grad{n}",
            [docs] + near(queries, attended[n], output_grad, gain, sums, other, *after),
            [half16, message], flops=mm,
        )

    def back(c, query_grad, after):
        n = c // 2
        ins = near(queries, keys[n], values[n], ag[n], state[n], after)
        ins += [(HBM, query_grad)] if c else []
        ins += near(*attended, gain, sums, other) if c == 1 else []
        outs = [(HBM, (tokens, width), BF), quarter32, quarter32]
        return call(
            functools.partial(back_kernel, c, hh, full), f"back{c}", ins, [outs[0]] + outs if c == 1 else outs,
            scratch=[
                pltpu.VMEM((tokens, hw // 2), BF), pltpu.SemaphoreType.DMA((hh // 2,)),
                pltpu.VMEM((tokens, width), BF), pltpu.SemaphoreType.DMA(()),
            ],
            aliases={6: int(c == 1)} if c else None, flops=7 * mm // 2,
        )

    way0, way1 = routes(seq, head, -1)
    ag0, bg0 = grad(0)
    ag = [ag0]
    got1 = [send(bg0, way0[0])]
    query_grad, kin0, vin0 = back(0, None, bg0)
    ag1, bg1 = grad(1, kin0)
    ag.append(ag1)
    bg = [bg0, bg1]
    got1.append(send(bg1, way1[0]))
    on0 = join(0, 1, bg[0], got1[0], bg1)
    got2a = send(on0, way0[1])
    normed, query_grad, kin1, vin1 = back(1, query_grad, on0)
    on1 = join(1, 1, bg[1], got1[1], kin1)
    got2b = send(on1, way1[1])
    query_grad, kin2, vin2 = back(2, query_grad, on1)
    more0 = later(0, 1, way0, bg[0], on0, got2a, kin2)
    more1 = later(1, 1, way1, bg[1], on1, got2b, on1)
    query_grad, kin3, vin3 = back(3, query_grad, got2b)
    got = [(got1[0], got2a, *more0), (got1[1], got2b, *more1)]
    inside = [(kin0, kin1, vin0, vin1), (kin2, kin3, vin2, vin3)]
    grads = []
    for n in range(HALVES):
        grads = call(
            functools.partial(final_kernel, n, hh, len(got[n])), f"final{n}",
            [docs] + near(keys[n], values[n], *inside[n], *got[n], *grads),
            [(HBM, (tokens, width), BF)] * 2 if n else [half16] * 2,
            scratch=[pltpu.VMEM((tokens, hw), BF)] * 2 + [pltpu.SemaphoreType.DMA((hh + 2,))] if n else (),
            flops=2 * mm,
        )
    return normed, query_grad, *grads


def solution(mesh):
    rows = P(("groups", "seq"), "head")
    in_specs = (rows, rows, rows, rows, P("head"), P(("groups", "seq")))
    out_specs = (rows, rows, rows, rows)
    short = mesh.shape["seq"] == 8 and mesh.shape["head"] == 2

    def body(queries, key_vectors, value_vectors, output_grad, norm_gain, block_docs):
        one = block_docs.shape[0] == 1
        fn = block_body if short and one else general_body
        return fn(queries, key_vectors, value_vectors, output_grad, norm_gain, block_docs)

    return jax.shard_map(body, mesh=mesh, in_specs=in_specs, out_specs=out_specs, check_vma=False)
```
